768 devices in a mesh: src: 48 (over y_lo, z), tgt: 16 (over x, y_hi, core).
Axes of the slice: x: 4, y: 8 (y_hi: 2, y_lo: 4; y = y_hi * 4 + y_lo), z: 12, core: 2. Of those that a mesh axis runs over, the one named last changes fastest.
Arguments:
- particle_position: float32 [3, 294912], P(None, ('src', 'tgt')), may hold values from 0 to 1, as said below
- particle_strength: float32 [3, 294912], P(None, ('src', 'tgt')), may hold values from -6 to 6
- core_radius: float32 [1, 294912], P(None, ('src', 'tgt')), may hold values from 0.05 to 0.12
- boundary_points: float32 [3, 48, 1024], P(None, None, 'tgt'), may hold values from 0 to 1, as said below
- vorticity: float32 [48, 3, 1024, 128], P('src', None, 'tgt'), may hold values from -6 to 6
- swirl: float32 [48, 1024, 128], P('src', 'tgt'), may hold values from -0.5 to 0.5
- diffusivity: float32 [48, 1024, 128], P('src', 'tgt'), may hold values from 0.05 to 0.2
- intersection_source: int32 [48, 16, 9], P('src', 'tgt'), may hold values from 0 to 191
- intersection_target: int32 [48, 16, 9], P('src', 'tgt'), may hold values from -1 to 143, as said below
Outputs:
- wall_velocity: float32 [3, 48, 1024], P(None, 'src', 'tgt')
- grid_vorticity: float32 [48, 3, 1024, 128], P('src', None, 'tgt')
- new_strength: float32 [3, 294912], P(None, ('src', 'tgt'))
The draws below stay inside these ranges and needn't reach their ends.
Inputs may be any that keep to these rules, and one draw needn't show every extreme that they name: `particle_position`: every coordinate of every particle lies in [0, 1). `boundary_points`: point (z, a) has its first two coordinates in [0, 1) and its third in [z / 48, (z + 1) / 48). `intersection_target`: an entry of list (s, t) is -1 or owner * 9 + block, naming particle block block of device (s, owner). Live entries stand before the -1 entries. Over all lists of one src index each particle block of each device is named at most once. No list names one owner in more than 2 live entries, and some list names some owner in exactly 2; some list has 9 live entries.
All inputs are finite; a program needn't handle non-finite values.
Results may differ from the reference program's by a relative error of at most 0.0003.
Values sent between devices are 32-bit elements; how exact they have to be, the bound alone decides.
A program may use at most 32 MiB of HBM per device.

```python
import math
import jax
import jax.numpy as jnp
from jax import lax

P_DEV = 384
ZD = 1
AD = 64
NR = 128
SUBSTEPS = 3
NPART = 294912
NZ = 48
NA = 1024
DENSITY = 294912
PB = 9
GB = 192
N_SRC = 48
N_TGT = 16


def vertical_coordinate(key):
    return jax.random.uniform(jax.random.fold_in(key, 12), (1, NPART), jnp.float32)


def draw_particle_position(key, part):
    first = jax.random.fold_in(key, 11)
    across = jax.random.uniform(first, (2, NPART), jnp.float32)
    vertical = vertical_coordinate(key)
    return jnp.concatenate([across, vertical], axis=0).astype(jnp.float32)


def draw_particle_strength(key, part):
    vertical = vertical_coordinate(key)[0]
    phase = jax.random.uniform(jax.random.fold_in(key, 41), (), jnp.float32) * (2.0 * math.pi)
    noise_key = jax.random.fold_in(key, 42)
    noise = jax.random.normal(noise_key, (3, NPART), jnp.float32)
    amplitude = 8.0 / math.sqrt(DENSITY)
    turning = math.pi
    heading = phase + turning * vertical
    coherent = amplitude * jnp.stack([jnp.cos(heading), jnp.sin(heading), jnp.zeros_like(heading)])
    return jnp.clip(noise + coherent, -6.0, 6.0).astype(jnp.float32)


def draw_boundary_points(key, part):
    first = jax.random.fold_in(key, 21)
    second = jax.random.fold_in(key, 22)
    across = jax.random.uniform(first, (2, NZ, NA), jnp.float32)
    within = jax.random.uniform(second, (NZ, NA), jnp.float32)
    planes = jnp.arange(NZ, dtype=jnp.float32)[:, None]
    vertical = ((planes + within) / NZ)[None]
    return jnp.concatenate([across, vertical], axis=0).astype(jnp.float32)


def one_row(rowkey):
    subkeys = jax.random.split(rowkey, 4)
    senders_order = jax.random.permutation(subkeys[0], N_TGT)
    anchor = jax.random.randint(subkeys[1], (), 0, N_TGT)
    halfway = (PB + 1) // 2
    receivers = jnp.arange(N_TGT, dtype=jnp.int32)
    offsets = (anchor - receivers) % N_TGT
    forced = offsets < min(N_TGT, halfway)
    filled = jnp.minimum(PB, 2 * (offsets + N_TGT * ((halfway - 1 - offsets) // N_TGT)) + 2)
    loose = jax.random.randint(subkeys[2], (N_TGT,), 2, PB // 2 + 3)
    loads = jnp.where(forced, filled, jnp.minimum(loose, PB))
    block_keys = jax.random.split(subkeys[3], N_TGT)
    shuffled = jax.vmap(jax.random.permutation, in_axes=(0, None))(block_keys, PB)
    indices = jnp.arange(PB, dtype=jnp.int32)
    active = indices[None, :] < loads[:, None]
    senders = senders_order[(receivers[:, None] + indices[None, :] // 2) % N_TGT]
    codes = receivers[:, None] * PB + shuffled
    flat_active = active.reshape(-1)
    flat_senders = senders.reshape(-1)
    flat_codes = codes.reshape(-1)
    positions = jnp.arange(N_TGT * PB, dtype=jnp.int32)

    def per_sender(sender):
        chosen = flat_active & (flat_senders == sender)
        scores = jnp.where(chosen, positions, positions + N_TGT * PB)
        selection = jnp.argsort(scores)[:PB]
        return jnp.where(chosen[selection], flat_codes[selection], -1)
    return jax.vmap(per_sender)(receivers)


def draw_intersection_target(key, part):
    rowkeys = jax.random.split(jax.random.fold_in(key, 31), N_SRC)
    return jax.vmap(one_row)(rowkeys).astype(jnp.int32)


def with_ends(result, key, low, top_value):
    longest = result.shape.index(max(result.shape))
    spots = []
    for shift in (0, 1):
        where = [jax.random.randint(jax.random.fold_in(key, axis), (), 0, length) for axis, length in enumerate(result.shape)]
        where[longest] = (where[longest] + shift) % result.shape[longest]
        spots.append(tuple(where))
    return result.at[spots[0]].set(low).at[spots[1]].set(top_value)


def level_of(key, shape, cuts, least, top_value):
    def one(dim, blocks):
        draws = jax.random.uniform(jax.random.fold_in(jax.random.fold_in(key, 6), dim), (blocks,), jnp.float32, least / len(cuts), top_value / len(cuts))
        return jnp.repeat(jnp.exp(draws), shape[dim] // blocks).reshape((-1,) + (1,) * (len(shape) - dim - 1))

    loudness = one(*cuts[0])
    for cut in cuts[1:]:
        loudness = loudness * one(*cut)
    return loudness


def scatter_about(rng, shape, deviation, reach, cuts=(), held_as=jnp.bfloat16):
    result = deviation * jax.random.normal(rng, shape, jnp.float32)
    if cuts:
        result = result * level_of(rng, shape, cuts, -0.22, 0.18)
    return jnp.clip(result, -reach, reach).astype(held_as)


def setup_inputs(seed: int = 0) -> dict:
    arg_keys = jax.random.split(jax.random.key(seed), 10)
    particle_position = draw_particle_position(jax.random.fold_in(arg_keys[9], 71), 0)
    particle_strength = draw_particle_strength(jax.random.fold_in(arg_keys[9], 71), 0)
    core_radius = jnp.clip(jnp.exp(math.log(0.12) - 0.8754687 * jax.random.uniform(arg_keys[2], (1, NPART), jnp.float32) ** level_of(arg_keys[2], (1, NPART), ((1, 768),), -0.2, 0.2)), 0.05, 0.12)
    boundary_points = draw_boundary_points(jax.random.fold_in(arg_keys[9], 71), 0)
    vorticity = scatter_about(arg_keys[4], (NZ, 3, NA, NR), 1.0, 6.0, ((0, 48), (2, 16)), jnp.float32)
    swirl = jnp.clip(jax.random.uniform(arg_keys[5], (NZ, NA, NR), jnp.float32, -0.5, 0.5) * level_of(arg_keys[5], (NZ, NA, NR), ((0, 48), (1, 16)), -0.4, 0.0), -0.5, 0.5)
    diffusivity = jnp.clip(0.05 + 0.15 * jax.random.uniform(arg_keys[6], (NZ, NA, NR), jnp.float32) ** level_of(arg_keys[6], (NZ, NA, NR), ((0, 48), (1, 16)), -0.2, 0.2), 0.05, 0.2)
    intersection_source = with_ends(jax.random.randint(arg_keys[7], (N_SRC, N_TGT, PB), 0, GB), jax.random.fold_in(arg_keys[7], 1), 0, GB - 1).astype(jnp.int32)
    intersection_target = draw_intersection_target(jax.random.fold_in(arg_keys[9], 71), 0)
    return {"particle_position": particle_position, "particle_strength": particle_strength, "core_radius": core_radius, "boundary_points": boundary_points, "vorticity": vorticity, "swirl": swirl, "diffusivity": diffusivity, "intersection_source": intersection_source, "intersection_target": intersection_target}


swirl_gain = 0.2

def divisor(number, limit):
    return max([candidate for candidate in range(1, min(number, limit) + 1) if number % candidate == 0])

def induced(targets, position, strength, radius):
    target_total = targets.shape[1]
    particle_total = position.shape[1]
    particle_step = divisor(particle_total, 2048)
    target_step = divisor(target_total, max(256, (1 << 22) // particle_step))
    target_blocks = targets.reshape(3, target_total // target_step, target_step).transpose(1, 0, 2)
    packed = jnp.concatenate([position, strength, radius], axis=0)
    particle_blocks = packed.reshape(7, particle_total // particle_step, particle_step).transpose(1, 0, 2)

    def per_target(target_block):

        def absorb(running_sum, particle_block):
            delta_x = target_block[0][:, None] - particle_block[0][None, :]
            delta_y = target_block[1][:, None] - particle_block[1][None, :]
            delta_z = target_block[2][:, None] - particle_block[2][None, :]
            distance = delta_x * delta_x + delta_y * delta_y + delta_z * delta_z + (particle_block[6] * particle_block[6])[None, :]
            inverse = lax.rsqrt(distance)
            weight = inverse * inverse * inverse
            along_x = particle_block[3][None, :]
            along_y = particle_block[4][None, :]
            along_z = particle_block[5][None, :]
            velocity_x = lax.optimization_barrier(jnp.sum(weight * (along_y * delta_z - along_z * delta_y), axis=1))
            velocity_y = lax.optimization_barrier(jnp.sum(weight * (along_z * delta_x - along_x * delta_z), axis=1))
            velocity_z = lax.optimization_barrier(jnp.sum(weight * (along_x * delta_y - along_y * delta_x), axis=1))
            return (running_sum + jnp.stack([velocity_x, velocity_y, velocity_z]), None)
        running_sum, unused = lax.scan(absorb, jnp.zeros((3, target_step), jnp.float32), particle_blocks)
        return running_sum
    blocked = lax.map(per_target, target_blocks)
    return blocked.transpose(1, 0, 2).reshape(3, target_total)

def substep(field, wall_ghost, local_swirl, local_diff):
    eastern = jnp.roll(field, -1, axis=2)
    western = jnp.roll(field, 1, axis=2)
    outward = jnp.concatenate([field[..., 1:], jnp.zeros_like(field[..., :1])], axis=3)
    inward = jnp.concatenate([wall_ghost[..., None], field[..., :-1]], axis=3)
    transport = local_swirl + swirl_gain * field[:, 2]
    return field + local_diff[:, None] * (eastern + western + outward + inward - 4.0 * field) - 0.5 * transport[:, None] * (eastern - western)

def reference(particle_position, particle_strength, core_radius, boundary_points, vorticity, swirl, diffusivity, intersection_source, intersection_target):
    prefactor = 1.6 / (4.0 * math.pi * math.sqrt(DENSITY))
    targets = boundary_points.reshape(3, NZ * NA)
    wall_speed = (induced(targets, particle_position, particle_strength, core_radius) * prefactor).reshape(3, NZ, NA)
    wall_ghost = wall_speed.transpose(1, 0, 2)
    field = vorticity
    for counter in range(SUBSTEPS):
        field = substep(field, wall_ghost, swirl, diffusivity)
    grid_blocks = field.reshape(N_SRC, ZD, 3, N_TGT, AD, NR).transpose(0, 3, 1, 2, 4, 5).reshape(N_SRC, N_TGT, GB, NR)
    rows_src = jnp.arange(N_SRC, dtype=jnp.int32)[:, None, None]
    rows_tgt = jnp.arange(N_TGT, dtype=jnp.int32)[None, :, None]
    picked = grid_blocks[rows_src, rows_tgt, intersection_source].reshape(N_SRC, N_TGT * PB, NR)
    labels = intersection_target.reshape(N_SRC, N_TGT * PB)
    matches = labels[:, None, :] == jnp.arange(N_TGT * PB, dtype=jnp.int32)[None, :, None]
    incoming = jnp.einsum('sde,sen->sdn', matches.astype(jnp.float32), picked.astype(jnp.float32), precision=lax.Precision.HIGHEST)
    covered = jnp.any(matches, axis=2)
    current = particle_strength.reshape(3, N_SRC, N_TGT, P_DEV // NR, NR).transpose(1, 2, 0, 3, 4).reshape(N_SRC, N_TGT * PB, NR)
    renewed = jnp.where(covered[..., None], incoming, current)
    new_strength = renewed.reshape(N_SRC, N_TGT, 3, P_DEV // NR, NR).transpose(2, 0, 1, 3, 4).reshape(3, NPART)
    return (wall_speed, field, new_strength)
```

```python
import math

import jax
import jax.numpy as jnp
from jax import lax
from jax.experimental import pallas as pl
from jax.experimental.pallas import tpu as pltpu
from jax.sharding import PartitionSpec as P

SUBSTEPS = 3
SWIRL_GAIN = 0.2
MESH = pl.DeviceIdType.MESH
F32 = jnp.float32
BF16 = jnp.bfloat16

NY, NZ = 4, 12
NX = 4
NT = 16
PART = 384
ANG = 64
RAD = 128
COLS = NY * NZ * ANG
GROUP = NZ * ANG
TILES = GROUP // 128
HALF = COLS // 2
BATCH = 2 * PART
GRAY = (0, 1, 3, 2)
BACK = (0, 2, 1, 3)


def peer(t, k):
    h, j, c = k // 8, (k // 2) % 4, k % 2
    x, hi, core = t // 4, (t // 2) % 2, t % 2
    return ((x + GRAY[j]) % NX) * 4 + ((hi + h) % 2) * 2 + (core + c) % 2


def back(k):
    return (k // 8) * 8 + BACK[(k // 2) % 4] * 2 + k % 2


def split(value):
    high = value.astype(BF16).astype(F32)
    rest = value - high
    middle = rest.astype(BF16).astype(F32)
    return high, middle, rest - middle


def kernel(
    prefactor,
    rows_ref,
    x_ref,
    a_ref,
    strength_ref,
    vort_ref,
    swirl_ref,
    diff_ref,
    wall_ref,
    field_ref,
    new_ref,
    chunk,
    tmat,
    pmat,
    fmat,
    acc,
    ext,
    vst,
    vr1,
    vs2,
    vr2,
    edge,
    edge_in,
    fin,
    rs,
    rr,
    g_send,
    g_recv,
    loc,
    h_send,
    h_recv,
    y_send,
    y_recv,
    z_send,
    z_recv,
    e_send,
    e_recv,
    r_send,
    r_recv,
):
    s = lax.axis_index("src")
    t = lax.axis_index("tgt")
    y, z = s // NZ, s % NZ
    left, right = (t + NT - 1) % NT, (t + 1) % NT

    barrier = pltpu.get_barrier_semaphore()
    for k in range(1, NT):
        pl.semaphore_signal(
            barrier, inc=1, device_id={"src": s, "tgt": peer(t, k)}, device_id_type=MESH
        )
    for d in range(1, NY):
        pl.semaphore_signal(
            barrier,
            inc=1,
            device_id={"src": ((y + d) % NY) * NZ + z, "tgt": t},
            device_id_type=MESH,
        )
    for d in range(1, NZ):
        pl.semaphore_signal(
            barrier,
            inc=1,
            device_id={"src": y * NZ + (z + d) % NZ, "tgt": t},
            device_id_type=MESH,
        )

    inner = [
        pltpu.make_async_copy(vort_ref, ext.at[0:3, 8:72], loc.at[0]),
        pltpu.make_async_copy(swirl_ref, ext.at[3, 8:72], loc.at[1]),
        pltpu.make_async_copy(diff_ref, ext.at[4, 8:72], loc.at[2]),
    ]
    for copy in inner:
        copy.start()

    gather = [
        pltpu.make_async_remote_copy(
            src_ref=a_ref,
            dst_ref=chunk.at[back(k)],
            send_sem=g_send.at[k],
            recv_sem=g_recv.at[back(k)],
            device_id={"src": s, "tgt": peer(t, k)},
            device_id_type=MESH,
        )
        for k in range(1, NT)
    ]
    halo = []
    for side, (to, rows, where) in enumerate(((right, 56, 0), (left, 0, 72))):
        for n, (src, dst) in enumerate(
            (
                (vort_ref.at[:, rows : rows + 8], ext.at[0:3, where : where + 8]),
                (swirl_ref.at[rows : rows + 8], ext.at[3, where : where + 8]),
                (diff_ref.at[rows : rows + 8], ext.at[4, where : where + 8]),
            )
        ):
            halo.append(
                pltpu.make_async_remote_copy(
                    src_ref=src,
                    dst_ref=dst,
                    send_sem=h_send.at[side * 3 + n],
                    recv_sem=h_recv.at[side * 3 + n],
                    device_id={"src": s, "tgt": to},
                    device_id_type=MESH,
                )
            )

    high, middle, low = split(x_ref[...])
    none = jnp.zeros_like(high)
    tmat[...] = jnp.concatenate([high, middle, low, high, middle, high, none, none], axis=0).astype(
        BF16
    )
    acc[...] = jnp.zeros_like(acc)
    chunk[0] = a_ref[...]

    def prepare(k):
        block = chunk[k]
        row = lax.broadcasted_iota(jnp.int32, block.shape, 0)
        high, middle, low = split(jnp.where(row == 7, 1.0, block))
        none = jnp.zeros_like(high)
        stacked = jnp.concatenate([high, high, high, middle, middle, low, none, none], axis=0)
        where = pl.ds(pl.multiple_of(k * PART, PART), PART)
        pmat[where, :] = stacked.T.astype(BF16)
        p = [-0.5 * block[n : n + 1] for n in range(3)]
        q = [block[n : n + 1] for n in range(4, 7)]
        moment = [
            q[1] * p[2] - q[2] * p[1],
            q[2] * p[0] - q[0] * p[2],
            q[0] * p[1] - q[1] * p[0],
        ]
        factors = jnp.concatenate(q + moment + [jnp.zeros((2, PART), F32)], axis=0)
        coarse = factors.astype(BF16).astype(F32)
        fmat[:, where] = jnp.concatenate([coarse, factors - coarse], axis=0).astype(BF16)

    def absorb(total, where, points):
        squared = jnp.dot(pmat[where, :], points, preferred_element_type=F32)
        weight = lax.rsqrt(squared * squared * squared)
        coarse = weight.astype(BF16)
        fine = (weight - coarse.astype(F32)).astype(BF16)
        factors = fmat[:, where]
        return (
            total
            + jnp.dot(factors, coarse, preferred_element_type=F32)
            + jnp.dot(factors, fine, preferred_element_type=F32)
        )

    def first(k, carry):
        @pl.when(k == 1)
        def _():
            pl.semaphore_wait(barrier, NT - 1 + NY - 1 + NZ - 1)
            for copy in gather:
                copy.start()
            for copy in halo:
                copy.start()

        @pl.when(k > 0)
        def _():
            pltpu.make_async_copy(a_ref, chunk.at[k], g_recv.at[k]).wait()

        prepare(k)
        where = pl.ds(pl.multiple_of(k * PART, PART), PART)
        for part in range(2):
            cols = slice(part * HALF, (part + 1) * HALF)
            acc[:, cols] = absorb(acc[:, cols], where, tmat[:, cols])
        return carry

    lax.fori_loop(0, NT // 2, first, 0)

    def second(k, carry):
        pltpu.make_async_copy(a_ref, chunk.at[k], g_recv.at[k]).wait()
        prepare(k)
        return carry

    lax.fori_loop(NT // 2, NT, second, 0)

    def to_y(g):
        return pltpu.make_async_remote_copy(
            src_ref=vst.at[g],
            dst_ref=vr1.at[g],
            send_sem=y_send.at[g],
            recv_sem=y_recv.at[g],
            device_id={"src": ((y + g + 1) % NY) * NZ + z, "tgt": t},
            device_id_type=MESH,
        )

    def plane_group(g, carry):
        cols = pl.ds(pl.multiple_of(((y + g + 1) % NY) * GROUP, GROUP), GROUP)
        points = tmat[:, cols]

        def step(n, total):
            return absorb(total, pl.ds(pl.multiple_of(n * BATCH, BATCH), BATCH), points)

        total = lax.fori_loop(NT * PART // BATCH // 2, NT * PART // BATCH, step, acc[:, cols])
        both = total[0:8] + total[8:16]
        place = x_ref[:, cols]
        x = [place[n : n + 1] for n in range(3)]
        q = [both[n : n + 1] for n in range(3)]
        velocity = jnp.concatenate(
            [
                q[1] * x[2] - q[2] * x[1] - both[3:4],
                q[2] * x[0] - q[0] * x[2] - both[4:5],
                q[0] * x[1] - q[1] * x[0] - both[5:6],
                jnp.zeros((1, GROUP), F32),
            ],
            axis=0,
        )
        velocity = velocity * prefactor
        for n in range(TILES):
            vst[g, n] = velocity[:, n * 128 : (n + 1) * 128]

        @pl.when(g < NY - 1)
        def _():
            to_y(g).start()

        return carry

    lax.fori_loop(0, NY, plane_group, 0)

    for g in range(NY - 1):
        to_y(g).wait_recv()
    vs2[...] = vst[NY - 1] + vr1[0] + vr1[1] + vr1[2]
    across = []
    for d in range(1, NZ):
        to = (z + d) % NZ
        across.append(
            pltpu.make_async_remote_copy(
                src_ref=vs2.at[to // 2],
                dst_ref=vr2.at[d],
                send_sem=z_send.at[d],
                recv_sem=z_recv.at[d],
                device_id={"src": y * NZ + to, "tgt": t},
                device_id_type=MESH,
            )
        )
    for copy in across:
        copy.start()
    for copy in inner:
        copy.wait()
    for copy in halo:
        copy.wait_recv()
    vr2[0] = vs2[z // 2]
    for copy in across:
        copy.wait_recv()
    pair = vr2[0]
    for d in range(1, NZ):
        pair = pair + vr2[d]
    odd = (z % 2).astype(F32)
    own = pair * (1.0 - odd) + pltpu.roll(pair, 64, 1) * odd
    wall_ref[...] = own[0:3, 0:ANG]
    edge[...] = own
    edges = [
        pltpu.make_async_remote_copy(
            src_ref=edge,
            dst_ref=edge_in.at[n],
            send_sem=e_send.at[n],
            recv_sem=e_recv.at[n],
            device_id={"src": s, "tgt": to},
            device_id_type=MESH,
        )
        for n, to in enumerate((right, left))
    ]
    for copy in edges:
        copy.start()
    for copy in edges:
        copy.wait_recv()
    lane4 = lax.broadcasted_iota(jnp.int32, (4, 128), 1)
    before = pltpu.roll(edge_in[0], 72, 1)
    after = pltpu.roll(edge_in[1], 72, 1)
    ghosts = jnp.where(lane4 < 8, before, jnp.where(lane4 < 72, pltpu.roll(own, 8, 1), after))
    ghosts = jnp.where(lane4 < 80, ghosts, 0.0)
    upright = jnp.concatenate([ghosts, jnp.zeros((124, 128), F32)], axis=0).T

    lane = lax.broadcasted_iota(jnp.int32, (80, RAD), 1)
    ghost = [jnp.broadcast_to(upright[0:80, m : m + 1], (80, RAD)) for m in range(3)]
    local_swirl, local_diff = ext[3], ext[4]
    w = [ext[0], ext[1], ext[2]]
    for _ in range(SUBSTEPS):
        half = 0.5 * (local_swirl + SWIRL_GAIN * w[2])
        moved = []
        for m in range(3):
            east = pltpu.roll(w[m], 79, 0)
            west = pltpu.roll(w[m], 1, 0)
            outward = jnp.where(lane == RAD - 1, 0.0, pltpu.roll(w[m], RAD - 1, 1))
            inward = jnp.where(lane == 0, ghost[m], pltpu.roll(w[m], 1, 1))
            moved.append(
                w[m]
                + local_diff * (east + west + outward + inward - 4.0 * w[m])
                - half * (east - west)
            )
        w = moved
    for m in range(3):
        fin[m * ANG : (m + 1) * ANG] = w[m][8:72]

    for k in range(NT):
        to = peer(t, k)
        for n in range(2):
            picked = fin[pl.ds(rows_ref[2 * to + n], 1), :]
            if k == 0:
                rr[0, n : n + 1] = picked
            else:
                rs[k, n : n + 1] = picked
    rows = [
        pltpu.make_async_remote_copy(
            src_ref=rs.at[k],
            dst_ref=rr.at[back(k)],
            send_sem=r_send.at[k],
            recv_sem=r_recv.at[back(k)],
            device_id={"src": s, "tgt": peer(t, k)},
            device_id_type=MESH,
        )
        for k in range(1, NT)
    ]
    for copy in rows:
        copy.start()
    for m in range(3):
        field_ref[m] = fin[m * ANG : (m + 1) * ANG]

    notes = jnp.concatenate([chunk[k, 7:8, 0:128] for k in range(NT)], axis=0)
    lane16 = lax.broadcasted_iota(jnp.int32, (NT, 128), 1)
    label = [
        jnp.sum(jnp.where(lane16 == 2 * t + n, notes, 0.0), axis=1, keepdims=True) for n in range(2)
    ]
    for copy in rows:
        copy.wait_recv()
    value = [rr[:, n] for n in range(2)]
    for b in range(9):
        hit = [label[n] == b + 1.0 for n in range(2)]
        came = sum(
            jnp.sum(jnp.where(hit[n], value[n], 0.0), axis=0, keepdims=True) for n in range(2)
        )
        count = sum(
            jnp.sum(jnp.where(hit[n], jnp.ones((NT, 128), F32), 0.0), axis=0, keepdims=True)
            for n in range(2)
        )
        place = slice((b % 3) * RAD, (b % 3 + 1) * RAD)
        old = strength_ref[b // 3 : b // 3 + 1, place]
        new_ref[b // 3 : b // 3 + 1, place] = jnp.where(count > 0.0, came, old)

    for copy in gather + halo + across + edges + rows:
        copy.wait_send()
    for g in range(NY - 1):
        to_y(g).wait_send()


def on_device(
    particle_position,
    particle_strength,
    core_radius,
    boundary_points,
    vorticity,
    swirl,
    diffusivity,
    intersection_source,
    intersection_target,
):
    prefactor = 1.6 / (4.0 * math.pi * math.sqrt(PART * NT * NY * NZ))
    x = boundary_points.reshape(3, COLS) - 0.5
    xs = jnp.concatenate(
        [
            x,
            jnp.ones((1, COLS), F32),
            jnp.zeros((3, COLS), F32),
            jnp.sum(x * x, axis=0, keepdims=True),
        ],
        axis=0,
    )
    codes = intersection_target.reshape(-1)
    sources = intersection_source.reshape(-1)
    count = codes.shape[0]
    active = codes >= 0
    ids = jnp.arange(count, dtype=jnp.int32)
    owners = jnp.where(active, codes // 9, -1)
    earlier = (owners[None, :] == owners[:, None]) & (ids[None, :] < ids[:, None])
    slot = jnp.where(active, owners * 2 + jnp.sum(earlier.astype(jnp.int32), axis=1), -1)
    lanes = jnp.arange(PART, dtype=jnp.int32)
    chosen = slot[:, None] == lanes[None, :]
    notes = jnp.sum(jnp.where(chosen, (codes % 9 + 1)[:, None], 0), axis=0)
    rows = jnp.sum(jnp.where(chosen[:, 0:32], sources[:, None], 0), axis=0)
    p = particle_position - 0.5
    chunk = jnp.concatenate(
        [
            -2.0 * p,
            jnp.sum(p * p, axis=0, keepdims=True) + core_radius * core_radius,
            particle_strength,
            notes.astype(F32)[None],
        ],
        axis=0,
    )
    vmem = pl.BlockSpec(memory_space=pltpu.VMEM)
    anywhere = pl.BlockSpec(memory_space=pl.ANY)
    dma = pltpu.SemaphoreType.DMA
    wall, field, new = pl.pallas_call(
        lambda *refs: kernel(prefactor, *refs),
        out_shape=(
            jax.ShapeDtypeStruct((3, ANG), F32),
            jax.ShapeDtypeStruct((3, ANG, RAD), F32),
            jax.ShapeDtypeStruct((3, PART), F32),
        ),
        in_specs=[
            pl.BlockSpec(memory_space=pltpu.SMEM),
            vmem,
            vmem,
            vmem,
            anywhere,
            anywhere,
            anywhere,
        ],
        out_specs=(vmem, vmem, vmem),
        scratch_shapes=[
            pltpu.VMEM((NT, 8, PART), F32),
            pltpu.VMEM((64, COLS), BF16),
            pltpu.VMEM((NT * PART, 64), BF16),
            pltpu.VMEM((16, NT * PART), BF16),
            pltpu.VMEM((16, COLS), F32),
            pltpu.VMEM((5, 80, RAD), F32),
            pltpu.VMEM((NY, TILES, 4, 128), F32),
            pltpu.VMEM((NY - 1, TILES, 4, 128), F32),
            pltpu.VMEM((TILES, 4, 128), F32),
            pltpu.VMEM((NZ, 4, 128), F32),
            pltpu.VMEM((4, 128), F32),
            pltpu.VMEM((2, 4, 128), F32),
            pltpu.VMEM((3 * ANG, RAD), F32),
            pltpu.VMEM((NT, 2, RAD), F32),
            pltpu.VMEM((NT, 2, RAD), F32),
            dma((NT,)),
            dma((NT,)),
            dma((3,)),
            dma((6,)),
            dma((6,)),
            dma((NY - 1,)),
            dma((NY - 1,)),
            dma((NZ,)),
            dma((NZ,)),
            dma((2,)),
            dma((2,)),
            dma((NT,)),
            dma((NT,)),
        ],
        compiler_params=pltpu.CompilerParams(
            collective_id=0, has_side_effects=True, vmem_limit_bytes=48 << 20
        ),
        name="wake",
    )(
        rows,
        xs,
        chunk,
        particle_strength,
        vorticity.reshape(3, ANG, RAD),
        swirl.reshape(ANG, RAD),
        diffusivity.reshape(ANG, RAD),
    )
    return (wall.reshape(3, 1, ANG), field.reshape(1, 3, ANG, RAD), new)


def solution(mesh):
    in_specs = (
        P(None, ("src", "tgt")),
        P(None, ("src", "tgt")),
        P(None, ("src", "tgt")),
        P(None, None, "tgt"),
        P("src", None, "tgt", None),
        P("src", "tgt", None),
        P("src", "tgt", None),
        P("src", "tgt", None),
        P("src", "tgt", None),
    )
    out_specs = (P(None, "src", "tgt"), P("src", None, "tgt", None), P(None, ("src", "tgt")))
    return jax.shard_map(
        on_device, mesh=mesh, in_specs=in_specs, out_specs=out_specs, check_vma=False
    )
```

```python
import math

import jax
import jax.numpy as jnp
from jax import lax
from jax.experimental import pallas as pl
from jax.experimental.pallas import tpu as pltpu
from jax.sharding import PartitionSpec as P

SUBSTEPS = 3
SWIRL_GAIN = 0.2
MESH = pl.DeviceIdType.MESH
F32 = jnp.float32
BF16 = jnp.bfloat16

NY, NZ = 4, 12
NX = 4
NT = 16
PART = 384
ANG = 64
RAD = 128
COLS = NY * NZ * ANG
GROUP = NZ * ANG
TILES = GROUP // 128
HALF = COLS // 2
BATCH = 2 * PART
GRAY = (0, 1, 3, 2)
BACK = (0, 2, 1, 3)


def peer(t, k):
    h, j, c = k // 8, (k // 2) % 4, k % 2
    x, hi, core = t // 4, (t // 2) % 2, t % 2
    return ((x + GRAY[j]) % NX) * 4 + ((hi + h) % 2) * 2 + (core + c) % 2


def back(k):
    return (k // 8) * 8 + BACK[(k // 2) % 4] * 2 + k % 2


def split(value):
    high = value.astype(BF16).astype(F32)
    rest = value - high
    middle = rest.astype(BF16).astype(F32)
    return high, middle, rest - middle


def kernel(
    prefactor,
    codes_ref,
    sources_ref,
    position_ref,
    force_ref,
    radius_ref,
    points_ref,
    vort_ref,
    swirl_ref,
    diff_ref,
    wall_ref,
    field_ref,
    new_ref,
    pos,
    strength_ref,
    radius,
    points_in,
    x_ref,
    pick,
    chunk,
    tmat,
    pmat,
    fmat,
    acc,
    ext,
    vst,
    vr1,
    vs2,
    vr2,
    edge,
    edge_in,
    fin,
    rs,
    rr,
    g_send,
    g_recv,
    loc,
    h_send,
    h_recv,
    y_send,
    y_recv,
    z_send,
    z_recv,
    e_send,
    e_recv,
    r_send,
    r_recv,
):
    s = lax.axis_index("src")
    t = lax.axis_index("tgt")
    y, z = s // NZ, s % NZ
    left, right = (t + NT - 1) % NT, (t + 1) % NT
    loads = [
        pltpu.make_async_copy(points_ref, points_in, loc.at[3]),
        pltpu.make_async_copy(position_ref, pos, loc.at[4]),
        pltpu.make_async_copy(force_ref, strength_ref, loc.at[5]),
        pltpu.make_async_copy(radius_ref, radius, loc.at[6]),
    ]
    for copy in loads:
        copy.start()

    friends = [{"src": s, "tgt": peer(t, k)} for k in range(1, NT)]
    friends += [{"src": ((y + d) % NY) * NZ + z, "tgt": t} for d in range(1, NY)]
    friends += [{"src": y * NZ + (z + d) % NZ, "tgt": t} for d in range(1, NZ)]
    barrier = pltpu.get_barrier_semaphore()

    for friend in friends:
        pl.semaphore_signal(barrier, inc=1, device_id=friend, device_id_type=MESH)

    inner = [
        pltpu.make_async_copy(vort_ref, ext.at[0:3, 8:72], loc.at[0]),
        pltpu.make_async_copy(swirl_ref, ext.at[3, 8:72], loc.at[1]),
        pltpu.make_async_copy(diff_ref, ext.at[4, 8:72], loc.at[2]),
    ]
    for copy in inner:
        copy.start()

    gather = [
        pltpu.make_async_remote_copy(
            src_ref=chunk.at[0],
            dst_ref=chunk.at[back(k)],
            send_sem=g_send.at[k],
            recv_sem=g_recv.at[back(k)],
            device_id={"src": s, "tgt": peer(t, k)},
            device_id_type=MESH,
        )
        for k in range(1, NT)
    ]
    halo = []
    for side, (to, rows, where) in enumerate(((right, 56, 0), (left, 0, 72))):
        for n, (src, dst) in enumerate(
            (
                (vort_ref.at[:, rows : rows + 8], ext.at[0:3, where : where + 8]),
                (swirl_ref.at[rows : rows + 8], ext.at[3, where : where + 8]),
                (diff_ref.at[rows : rows + 8], ext.at[4, where : where + 8]),
            )
        ):
            halo.append(
                pltpu.make_async_remote_copy(
                    src_ref=src,
                    dst_ref=dst,
                    send_sem=h_send.at[side * 3 + n],
                    recv_sem=h_recv.at[side * 3 + n],
                    device_id={"src": s, "tgt": to},
                    device_id_type=MESH,
                )
            )

    codes = [codes_ref[i] for i in range(9)]
    owners = [jnp.where(code >= 0, code // 9, -1) for code in codes]
    slots = []
    for i in range(9):
        rank = jnp.int32(0)
        for j in range(i):
            rank = rank + jnp.where(owners[j] == owners[i], 1, 0)
        slots.append(jnp.where(codes[i] >= 0, owners[i] * 2 + rank, -1))
    lane1 = lax.broadcasted_iota(jnp.int32, (1, 128), 1)
    notes = jnp.zeros((1, 128), jnp.int32)
    for i in range(9):
        notes = jnp.where(lane1 == slots[i], codes[i] % 9 + 1, notes)
    for k in range(NT):
        for n in range(2):
            row = jnp.int32(0)
            for i in range(9):
                row = jnp.where(slots[i] == 2 * peer(t, k) + n, sources_ref[i], row)
            pick[2 * k + n] = row

    loads[0].wait()
    pairs = []
    for m in range(3):
        even = points_in[m, pl.ds(0, NY * NZ // 2, stride=2), :]
        odd_ones = points_in[m, pl.ds(1, NY * NZ // 2, stride=2), :]
        pairs.append(jnp.concatenate([even, odd_ones], axis=1) - 0.5)
    square = pairs[0] * pairs[0] + pairs[1] * pairs[1] + pairs[2] * pairs[2]
    for q in range(COLS // 128):
        x_ref[:, q * 128 : (q + 1) * 128] = jnp.concatenate(
            [pairs[m][q : q + 1] for m in range(3)]
            + [jnp.ones((1, 128), F32), jnp.zeros((3, 128), F32), square[q : q + 1]],
            axis=0,
        )
    high, middle, low = split(x_ref[...])
    none = jnp.zeros_like(high)
    tmat[...] = jnp.concatenate([high, middle, low, high, middle, high, none, none], axis=0).astype(
        BF16
    )
    acc[...] = jnp.zeros_like(acc)
    for copy in loads[1:]:
        copy.wait()
    centred = [pos[m : m + 1] - 0.5 for m in range(3)]
    core = radius[...]
    chunk[0] = jnp.concatenate(
        [-2.0 * c for c in centred]
        + [
            centred[0] * centred[0]
            + centred[1] * centred[1]
            + centred[2] * centred[2]
            + core * core
        ]
        + [strength_ref[m : m + 1] for m in range(3)]
        + [jnp.concatenate([notes.astype(F32), jnp.zeros((1, PART - 128), F32)], axis=1)],
        axis=0,
    )

    def factor(block, p_out, f_out):
        size = block.shape[1]
        row = lax.broadcasted_iota(jnp.int32, block.shape, 0)
        high, middle, low = split(jnp.where(row == 7, 1.0, block))
        none = jnp.zeros_like(high)
        stacked = jnp.concatenate([high, high, high, middle, middle, low, none, none], axis=0)
        p_out[...] = stacked.T.astype(BF16)
        p = [-0.5 * block[n : n + 1] for n in range(3)]
        q = [block[n : n + 1] for n in range(4, 7)]
        moment = [
            q[1] * p[2] - q[2] * p[1],
            q[2] * p[0] - q[0] * p[2],
            q[0] * p[1] - q[1] * p[0],
        ]
        factors = jnp.concatenate(q + moment + [jnp.zeros((2, size), F32)], axis=0)
        coarse = factors.astype(BF16).astype(F32)
        f_out[...] = jnp.concatenate([coarse, factors - coarse], axis=0).astype(BF16)

    def span(n):
        return pl.ds(pl.multiple_of(n * PART, PART), PART)

    def prepare(n):
        factor(chunk[n], pmat.at[span(n)], fmat.at[:, span(n)])

    def absorb(total, p, factors, points):
        squared = jnp.dot(p, points, preferred_element_type=F32)
        weight = lax.rsqrt(squared * squared * squared)
        coarse = weight.astype(BF16)
        fine = (weight - coarse.astype(F32)).astype(BF16)
        return (
            total
            + jnp.dot(factors, coarse, preferred_element_type=F32)
            + jnp.dot(factors, fine, preferred_element_type=F32)
        )

    def absorb_all(p, factors):
        for part in range(2):
            cols = slice(part * HALF, (part + 1) * HALF)
            acc[:, cols] = absorb(acc[:, cols], p, factors, tmat[:, cols])

    factor(chunk[0], pmat.at[0:PART], fmat.at[:, 0:PART])
    absorb_all(pmat[0:PART, :], fmat[:, 0:PART])

    pl.semaphore_wait(barrier, len(friends))
    for copy in gather:
        copy.start()
    for copy in halo:
        copy.start()

    def first(n, carry):
        pltpu.make_async_copy(chunk.at[0], chunk.at[n], g_recv.at[n]).wait()
        prepare(n)
        absorb_all(pmat[span(n), :], fmat[:, span(n)])
        return carry

    lax.fori_loop(1, NT // 2, first, 0)

    def second(n, carry):
        pltpu.make_async_copy(chunk.at[0], chunk.at[n], g_recv.at[n]).wait()
        prepare(n)
        return carry

    lax.fori_loop(NT // 2, NT, second, 0)

    def to_y(g):
        return pltpu.make_async_remote_copy(
            src_ref=vst.at[g],
            dst_ref=vr1.at[g],
            send_sem=y_send.at[g],
            recv_sem=y_recv.at[g],
            device_id={"src": ((y + g + 1) % NY) * NZ + z, "tgt": t},
            device_id_type=MESH,
        )

    def plane_group(g, carry):
        cols = pl.ds(pl.multiple_of(((y + g + 1) % NY) * GROUP, GROUP), GROUP)
        points = tmat[:, cols]

        def step(n, total):
            where = pl.ds(pl.multiple_of(n * BATCH, BATCH), BATCH)
            return absorb(total, pmat[where, :], fmat[:, where], points)

        batches = NT * PART // BATCH
        total = lax.fori_loop(batches // 2, batches, step, acc[:, cols])
        both = total[0:8] + total[8:16]
        place = x_ref[:, cols]
        x = [place[n : n + 1] for n in range(3)]
        q = [both[n : n + 1] for n in range(3)]
        velocity = jnp.concatenate(
            [
                q[1] * x[2] - q[2] * x[1] - both[3:4],
                q[2] * x[0] - q[0] * x[2] - both[4:5],
                q[0] * x[1] - q[1] * x[0] - both[5:6],
                jnp.zeros((1, GROUP), F32),
            ],
            axis=0,
        )
        velocity = velocity * prefactor
        for n in range(TILES):
            vst[g, n] = velocity[:, n * 128 : (n + 1) * 128]

        @pl.when(g < NY - 1)
        def _():
            to_y(g).start()

        return carry

    lax.fori_loop(0, NY, plane_group, 0)

    for g in range(NY - 1):
        to_y(g).wait_recv()
    vs2[...] = vst[NY - 1] + vr1[0] + vr1[1] + vr1[2]
    across = []
    for d in range(1, NZ):
        to = (z + d) % NZ
        across.append(
            pltpu.make_async_remote_copy(
                src_ref=vs2.at[to // 2],
                dst_ref=vr2.at[d],
                send_sem=z_send.at[d],
                recv_sem=z_recv.at[d],
                device_id={"src": y * NZ + to, "tgt": t},
                device_id_type=MESH,
            )
        )
    for copy in across:
        copy.start()
    for copy in inner:
        copy.wait()
    for copy in halo:
        copy.wait_recv()
    vr2[0] = vs2[z // 2]
    for copy in across:
        copy.wait_recv()
    pair = vr2[0]
    for d in range(1, NZ):
        pair = pair + vr2[d]
    odd = (z % 2).astype(F32)
    own = pair * (1.0 - odd) + pltpu.roll(pair, 64, 1) * odd
    wall_ref[...] = own[0:3, 0:ANG]
    edge[...] = own
    edges = [
        pltpu.make_async_remote_copy(
            src_ref=edge,
            dst_ref=edge_in.at[n],
            send_sem=e_send.at[n],
            recv_sem=e_recv.at[n],
            device_id={"src": s, "tgt": to},
            device_id_type=MESH,
        )
        for n, to in enumerate((right, left))
    ]
    for copy in edges:
        copy.start()
    for copy in edges:
        copy.wait_recv()
    lane4 = lax.broadcasted_iota(jnp.int32, (4, 128), 1)
    before = pltpu.roll(edge_in[0], 72, 1)
    after = pltpu.roll(edge_in[1], 72, 1)
    ghosts = jnp.where(lane4 < 8, before, jnp.where(lane4 < 72, pltpu.roll(own, 8, 1), after))
    ghosts = jnp.where(lane4 < 80, ghosts, 0.0)
    upright = jnp.concatenate([ghosts, jnp.zeros((124, 128), F32)], axis=0).T

    lane = lax.broadcasted_iota(jnp.int32, (80, RAD), 1)
    ghost = [jnp.broadcast_to(upright[0:80, m : m + 1], (80, RAD)) for m in range(3)]
    local_swirl, local_diff = ext[3], ext[4]
    w = [ext[0], ext[1], ext[2]]
    for _ in range(SUBSTEPS):
        half = 0.5 * (local_swirl + SWIRL_GAIN * w[2])
        moved = []
        for m in range(3):
            east = pltpu.roll(w[m], 79, 0)
            west = pltpu.roll(w[m], 1, 0)
            outward = jnp.where(lane == RAD - 1, 0.0, pltpu.roll(w[m], RAD - 1, 1))
            inward = jnp.where(lane == 0, ghost[m], pltpu.roll(w[m], 1, 1))
            moved.append(
                w[m]
                + local_diff * (east + west + outward + inward - 4.0 * w[m])
                - half * (east - west)
            )
        w = moved
    for m in range(3):
        fin[m * ANG : (m + 1) * ANG] = w[m][8:72]

    for k in range(NT):
        for n in range(2):
            picked = fin[pl.ds(pick[2 * k + n], 1), :]
            if k == 0:
                rr[0, n : n + 1] = picked
            else:
                rs[k, n : n + 1] = picked
    rows = [
        pltpu.make_async_remote_copy(
            src_ref=rs.at[k],
            dst_ref=rr.at[back(k)],
            send_sem=r_send.at[k],
            recv_sem=r_recv.at[back(k)],
            device_id={"src": s, "tgt": peer(t, k)},
            device_id_type=MESH,
        )
        for k in range(1, NT)
    ]
    for copy in rows:
        copy.start()
    for m in range(3):
        field_ref[m] = fin[m * ANG : (m + 1) * ANG]

    notes = jnp.concatenate([chunk[k, 7:8, 0:128] for k in range(NT)], axis=0)
    lane16 = lax.broadcasted_iota(jnp.int32, (NT, 128), 1)
    label = [
        jnp.sum(jnp.where(lane16 == 2 * t + n, notes, 0.0), axis=1, keepdims=True) for n in range(2)
    ]
    for copy in rows:
        copy.wait_recv()
    value = [rr[:, n] for n in range(2)]
    for b in range(9):
        hit = [label[n] == b + 1.0 for n in range(2)]
        came = sum(
            jnp.sum(jnp.where(hit[n], value[n], 0.0), axis=0, keepdims=True) for n in range(2)
        )
        count = sum(
            jnp.sum(jnp.where(hit[n], jnp.ones((NT, 128), F32), 0.0), axis=0, keepdims=True)
            for n in range(2)
        )
        place = slice((b % 3) * RAD, (b % 3 + 1) * RAD)
        old = strength_ref[b // 3 : b // 3 + 1, place]
        new_ref[b // 3 : b // 3 + 1, place] = jnp.where(count > 0.0, came, old)

    for copy in gather + halo + across + edges + rows:
        copy.wait_send()
    for g in range(NY - 1):
        to_y(g).wait_send()


def on_device(
    particle_position,
    particle_strength,
    core_radius,
    boundary_points,
    vorticity,
    swirl,
    diffusivity,
    intersection_source,
    intersection_target,
):
    prefactor = 1.6 / (4.0 * math.pi * math.sqrt(PART * NT * NY * NZ))
    vmem = pl.BlockSpec(memory_space=pltpu.VMEM)
    smem = pl.BlockSpec(memory_space=pltpu.SMEM)
    hbm = pl.BlockSpec(memory_space=pltpu.HBM)
    dma = pltpu.SemaphoreType.DMA
    wall, field, new = pl.pallas_call(
        lambda *refs: kernel(prefactor, *refs),
        out_shape=(
            jax.ShapeDtypeStruct((3, ANG), F32),
            jax.ShapeDtypeStruct((3, ANG, RAD), F32),
            jax.ShapeDtypeStruct((3, PART), F32),
        ),
        in_specs=[smem] * 2 + [hbm] * 7,
        out_specs=(vmem, vmem, vmem),
        scratch_shapes=[
            pltpu.VMEM((3, PART), F32),
            pltpu.VMEM((3, PART), F32),
            pltpu.VMEM((1, PART), F32),
            pltpu.VMEM((3, NY * NZ, ANG), F32),
            pltpu.VMEM((8, COLS), F32),
            pltpu.SMEM((2 * NT,), jnp.int32),
            pltpu.VMEM((NT, 8, PART), F32),
            pltpu.VMEM((64, COLS), BF16),
            pltpu.VMEM((NT * PART, 64), BF16),
            pltpu.VMEM((16, NT * PART), BF16),
            pltpu.VMEM((16, COLS), F32),
            pltpu.VMEM((5, 80, RAD), F32),
            pltpu.VMEM((NY, TILES, 4, 128), F32),
            pltpu.VMEM((NY - 1, TILES, 4, 128), F32),
            pltpu.VMEM((TILES, 4, 128), F32),
            pltpu.VMEM((NZ, 4, 128), F32),
            pltpu.VMEM((4, 128), F32),
            pltpu.VMEM((2, 4, 128), F32),
            pltpu.VMEM((3 * ANG, RAD), F32),
            pltpu.VMEM((NT, 2, RAD), F32),
            pltpu.VMEM((NT, 2, RAD), F32),
            dma((NT,)),
            dma((NT,)),
            dma((7,)),
            dma((6,)),
            dma((6,)),
            dma((NY - 1,)),
            dma((NY - 1,)),
            dma((NZ,)),
            dma((NZ,)),
            dma((2,)),
            dma((2,)),
            dma((NT,)),
            dma((NT,)),
        ],
        compiler_params=pltpu.CompilerParams(
            collective_id=0, has_side_effects=True, vmem_limit_bytes=67_000_000
        ),
        name="wake",
    )(
        intersection_target.reshape(-1),
        intersection_source.reshape(-1),
        particle_position,
        particle_strength,
        core_radius,
        boundary_points,
        vorticity.reshape(3, ANG, RAD),
        swirl.reshape(ANG, RAD),
        diffusivity.reshape(ANG, RAD),
    )
    return (wall.reshape(3, 1, ANG), field.reshape(1, 3, ANG, RAD), new)


def solution(mesh):
    in_specs = (
        P(None, ("src", "tgt")),
        P(None, ("src", "tgt")),
        P(None, ("src", "tgt")),
        P(None, None, "tgt"),
        P("src", None, "tgt", None),
        P("src", "tgt", None),
        P("src", "tgt", None),
        P("src", "tgt", None),
        P("src", "tgt", None),
    )
    out_specs = (P(None, "src", "tgt"), P("src", None, "tgt", None), P(None, ("src", "tgt")))
    return jax.shard_map(
        on_device, mesh=mesh, in_specs=in_specs, out_specs=out_specs, check_vma=False
    )
```

```python
import math

import jax
import jax.numpy as jnp
from jax import lax
from jax.experimental import pallas as pl
from jax.experimental.pallas import tpu as pltpu
from jax.sharding import PartitionSpec as P

SUBSTEPS = 3
SWIRL_GAIN = 0.2
MESH = pl.DeviceIdType.MESH
F32 = jnp.float32
BF16 = jnp.bfloat16

NY, NZ = 4, 12
NX = 4
NT = 16
PART = 384
ANG = 64
RAD = 128
COLS = NY * NZ * ANG
GROUP = NZ * ANG
TILES = GROUP // 128
HALF = COLS // 2
BATCH = 2 * PART
GRAY = (0, 1, 3, 2)
BACK = (0, 2, 1, 3)


def peer(t, k):
    h, j, c = k // 8, (k // 2) % 4, k % 2
    x, hi, core = t // 4, (t // 2) % 2, t % 2
    return ((x + GRAY[j]) % NX) * 4 + ((hi + h) % 2) * 2 + (core + c) % 2


def back(k):
    return (k // 8) * 8 + BACK[(k // 2) % 4] * 2 + k % 2


def split(value):
    high = value.astype(BF16).astype(F32)
    rest = value - high
    middle = rest.astype(BF16).astype(F32)
    return high, middle, rest - middle


def advance(w, carrier, local_swirl, local_diff, ghost, closed):
    lane = lax.broadcasted_iota(jnp.int32, w[0].shape, 1)
    for _ in range(SUBSTEPS):
        half = 0.5 * (local_swirl + SWIRL_GAIN * w[carrier])
        moved = []
        for value, wall in zip(w, ghost):
            east = pltpu.roll(value, value.shape[0] - 1, 0)
            west = pltpu.roll(value, 1, 0)
            outward = pltpu.roll(value, RAD - 1, 1)
            if closed:
                outward = jnp.where(lane == RAD - 1, 0.0, outward)
            inward = jnp.where(lane == 0, wall, pltpu.roll(value, 1, 1))
            moved.append(
                value
                + local_diff * (east + west + outward + inward - 4.0 * value)
                - half * (east - west)
            )
        w = moved
    return w


def kernel(
    prefactor,
    codes_ref,
    sources_ref,
    position_ref,
    force_ref,
    radius_ref,
    points_ref,
    vort_ref,
    swirl_ref,
    diff_ref,
    wall_ref,
    field_ref,
    new_ref,
    pos,
    strength_ref,
    radius,
    points_in,
    x_ref,
    pick,
    chunk,
    tmat,
    pmat,
    fmat,
    acc,
    ext,
    vst,
    vr1,
    vs2,
    vr2,
    edge,
    walls,
    listed,
    onehot,
    fin,
    rs,
    rr,
    g_send,
    g_recv,
    loc,
    h_send,
    h_recv,
    y_send,
    y_recv,
    z_send,
    z_recv,
    e_send,
    e_recv,
    r_send,
    r_recv,
):
    s = lax.axis_index("src")
    t = lax.axis_index("tgt")
    y, z = s // NZ, s % NZ
    left, right = (t + NT - 1) % NT, (t + 1) % NT
    loads = [
        pltpu.make_async_copy(points_ref, points_in, loc.at[3]),
        pltpu.make_async_copy(position_ref, pos, loc.at[4]),
        pltpu.make_async_copy(force_ref, strength_ref, loc.at[5]),
        pltpu.make_async_copy(radius_ref, radius, loc.at[6]),
    ]
    for copy in loads:
        copy.start()

    friends = [{"src": s, "tgt": peer(t, k)} for k in range(1, NT)]
    friends += [{"src": ((y + d) % NY) * NZ + z, "tgt": t} for d in range(1, NY)]
    friends += [{"src": y * NZ + (z + d) % NZ, "tgt": t} for d in range(1, NZ)]
    barrier = pltpu.get_barrier_semaphore()

    for friend in friends:
        pl.semaphore_signal(barrier, inc=1, device_id=friend, device_id_type=MESH)

    inner = [
        pltpu.make_async_copy(vort_ref, ext.at[0:3, 8:72], loc.at[0]),
        pltpu.make_async_copy(swirl_ref, ext.at[3, 8:72], loc.at[1]),
        pltpu.make_async_copy(diff_ref, ext.at[4, 8:72], loc.at[2]),
    ]
    for copy in inner:
        copy.start()

    gather = [
        pltpu.make_async_remote_copy(
            src_ref=chunk.at[0],
            dst_ref=chunk.at[back(k)],
            send_sem=g_send.at[k],
            recv_sem=g_recv.at[back(k)],
            device_id={"src": s, "tgt": peer(t, k)},
            device_id_type=MESH,
        )
        for k in range(1, NT)
    ]
    halo = []
    for side, (to, rows, where) in enumerate(((right, 56, 0), (left, 0, 72))):
        for n, (src, dst) in enumerate(
            (
                (vort_ref.at[:, rows : rows + 8], ext.at[0:3, where : where + 8]),
                (swirl_ref.at[rows : rows + 8], ext.at[3, where : where + 8]),
                (diff_ref.at[rows : rows + 8], ext.at[4, where : where + 8]),
            )
        ):
            halo.append(
                pltpu.make_async_remote_copy(
                    src_ref=src,
                    dst_ref=dst,
                    send_sem=h_send.at[side * 3 + n],
                    recv_sem=h_recv.at[side * 3 + n],
                    device_id={"src": s, "tgt": to},
                    device_id_type=MESH,
                )
            )

    codes = [codes_ref[i] for i in range(9)]
    owners = [jnp.where(code >= 0, code // 9, -1) for code in codes]
    slots = []
    for i in range(9):
        rank = jnp.int32(0)
        for j in range(i):
            rank = rank + jnp.where(owners[j] == owners[i], 1, 0)
        slots.append(jnp.where(codes[i] >= 0, owners[i] * 2 + rank, -1))
    for k in range(NT):
        for n in range(2):
            row, name = jnp.int32(0), jnp.int32(0)
            for i in range(9):
                here = slots[i] == 2 * peer(t, k) + n
                row = jnp.where(here, sources_ref[i], row)
                name = jnp.where(here, codes[i] % 9 + 1, name)
            pick[2 * k + n] = row
            pick[2 * NT + 2 * k + n] = name

    loads[0].wait()
    pairs = []
    for m in range(3):
        even = points_in[m, pl.ds(0, NY * NZ // 2, stride=2), :]
        odd_ones = points_in[m, pl.ds(1, NY * NZ // 2, stride=2), :]
        pairs.append(jnp.concatenate([even, odd_ones], axis=1) - 0.5)
    square = pairs[0] * pairs[0] + pairs[1] * pairs[1] + pairs[2] * pairs[2]
    for q in range(COLS // 128):
        x_ref[:, q * 128 : (q + 1) * 128] = jnp.concatenate(
            [pairs[m][q : q + 1] for m in range(3)]
            + [jnp.ones((1, 128), F32), jnp.zeros((3, 128), F32), square[q : q + 1]],
            axis=0,
        )
    high, middle, low = split(x_ref[...])
    none = jnp.zeros_like(high)
    tmat[...] = jnp.concatenate([high, middle, low, high, middle, high, none, none], axis=0).astype(
        BF16
    )
    acc[...] = jnp.zeros_like(acc)
    for copy in loads[1:]:
        copy.wait()
    centred = [pos[m : m + 1] - 0.5 for m in range(3)]
    core = radius[...]
    chunk[0] = jnp.concatenate(
        [-2.0 * c for c in centred]
        + [
            centred[0] * centred[0]
            + centred[1] * centred[1]
            + centred[2] * centred[2]
            + core * core
        ]
        + [strength_ref[m : m + 1] for m in range(3)]
        + [jnp.zeros((1, PART), F32)],
        axis=0,
    )

    def factor(block, p_out, f_out):
        size = block.shape[1]
        row = lax.broadcasted_iota(jnp.int32, block.shape, 0)
        high, middle, low = split(jnp.where(row == 7, 1.0, block))
        none = jnp.zeros_like(high)
        stacked = jnp.concatenate([high, high, high, middle, middle, low, none, none], axis=0)
        p_out[...] = stacked.T.astype(BF16)
        p = [-0.5 * block[n : n + 1] for n in range(3)]
        q = [block[n : n + 1] for n in range(4, 7)]
        moment = [
            q[1] * p[2] - q[2] * p[1],
            q[2] * p[0] - q[0] * p[2],
            q[0] * p[1] - q[1] * p[0],
        ]
        factors = jnp.concatenate(q + moment + [jnp.zeros((2, size), F32)], axis=0)
        coarse = factors.astype(BF16).astype(F32)
        f_out[...] = jnp.concatenate([coarse, factors - coarse], axis=0).astype(BF16)

    def span(n):
        return pl.ds(pl.multiple_of(n * PART, PART), PART)

    def prepare(n):
        factor(chunk[n], pmat.at[span(n)], fmat.at[:, span(n)])

    def absorb(total, p, factors, points):
        squared = jnp.dot(p, points, preferred_element_type=F32)
        weight = lax.rsqrt(squared * squared * squared)
        coarse = weight.astype(BF16)
        fine = (weight - coarse.astype(F32)).astype(BF16)
        return (
            total
            + jnp.dot(factors, coarse, preferred_element_type=F32)
            + jnp.dot(factors, fine, preferred_element_type=F32)
        )

    def absorb_all(p, factors):
        for part in range(2):
            cols = slice(part * HALF, (part + 1) * HALF)
            acc[:, cols] = absorb(acc[:, cols], p, factors, tmat[:, cols])

    factor(chunk[0], pmat.at[0:PART], fmat.at[:, 0:PART])
    absorb_all(pmat[0:PART, :], fmat[:, 0:PART])

    pl.semaphore_wait(barrier, len(friends))
    for copy in gather:
        copy.start()
    for copy in halo:
        copy.start()

    def first(n, carry):
        pltpu.make_async_copy(chunk.at[0], chunk.at[n], g_recv.at[n]).wait()
        prepare(n)
        absorb_all(pmat[span(n), :], fmat[:, span(n)])
        return carry

    lax.fori_loop(1, NT // 2, first, 0)

    for copy in inner:
        copy.wait()
    for copy in halo:
        copy.wait_recv()
    nothing = jnp.zeros((80, RAD), F32)
    w = advance([ext[0], ext[1], ext[2]], 2, ext[3], ext[4], [nothing] * 3, True)
    for m in range(3):
        fin[m * ANG : (m + 1) * ANG] = w[m][8:72]
    lane8 = lax.broadcasted_iota(jnp.int32, (8, RAD), 1)
    row8 = lax.broadcasted_iota(jnp.int32, (8, RAD), 0)

    def gather_row(n, carry):
        block = pick[n]
        m, a = block // ANG, block % ANG
        rows = pl.ds(a + 5, 8)
        tile = jnp.where(
            lane8 < 8,
            ext[m, rows, :],
            jnp.where(
                lane8 < 16,
                pltpu.roll(ext[2, rows, :], 8, 1),
                jnp.where(
                    lane8 < 24,
                    pltpu.roll(ext[3, rows, :], 16, 1),
                    pltpu.roll(ext[4, rows, :], 24, 1),
                ),
            ),
        )
        angle = (row8 + (t * ANG + a + NT * ANG - 3)) % (NT * ANG)
        tile = jnp.where(lane8 == 32, pick[2 * NT + n].astype(F32), tile)
        tile = jnp.where(lane8 == 33, m.astype(F32), tile)
        tile = jnp.where(lane8 == 34, angle.astype(F32), tile)
        rs[n] = jnp.where(row8 == 7, fin[pl.ds(block, 1), :], tile)
        return carry

    lax.fori_loop(0, 2 * NT, gather_row, 0)
    rr[0:2] = rs[0:2]
    rows = [
        pltpu.make_async_remote_copy(
            src_ref=rs.at[2 * k : 2 * k + 2],
            dst_ref=rr.at[2 * back(k) : 2 * back(k) + 2],
            send_sem=r_send.at[k],
            recv_sem=r_recv.at[back(k)],
            device_id={"src": s, "tgt": peer(t, k)},
            device_id_type=MESH,
        )
        for k in range(1, NT)
    ]
    for copy in rows:
        copy.start()

    def second(n, carry):
        pltpu.make_async_copy(chunk.at[0], chunk.at[n], g_recv.at[n]).wait()
        prepare(n)
        return carry

    lax.fori_loop(NT // 2, NT, second, 0)

    def to_y(g):
        return pltpu.make_async_remote_copy(
            src_ref=vst.at[g],
            dst_ref=vr1.at[g],
            send_sem=y_send.at[g],
            recv_sem=y_recv.at[g],
            device_id={"src": ((y + g + 1) % NY) * NZ + z, "tgt": t},
            device_id_type=MESH,
        )

    def plane_group(g, carry):
        cols = pl.ds(pl.multiple_of(((y + g + 1) % NY) * GROUP, GROUP), GROUP)
        points = tmat[:, cols]

        def step(n, total):
            where = pl.ds(pl.multiple_of(n * BATCH, BATCH), BATCH)
            return absorb(total, pmat[where, :], fmat[:, where], points)

        batches = NT * PART // BATCH
        total = lax.fori_loop(batches // 2, batches, step, acc[:, cols])
        both = total[0:8] + total[8:16]
        place = x_ref[:, cols]
        x = [place[n : n + 1] for n in range(3)]
        q = [both[n : n + 1] for n in range(3)]
        velocity = jnp.concatenate(
            [
                q[1] * x[2] - q[2] * x[1] - both[3:4],
                q[2] * x[0] - q[0] * x[2] - both[4:5],
                q[0] * x[1] - q[1] * x[0] - both[5:6],
                jnp.zeros((1, GROUP), F32),
            ],
            axis=0,
        )
        velocity = velocity * prefactor
        for n in range(TILES):
            vst[g, n] = velocity[:, n * 128 : (n + 1) * 128]

        @pl.when(g < NY - 1)
        def _():
            to_y(g).start()

        return carry

    lax.fori_loop(0, NY, plane_group, 0)

    for g in range(NY - 1):
        to_y(g).wait_recv()
    vs2[...] = vst[NY - 1] + vr1[0] + vr1[1] + vr1[2]
    across = []
    for d in range(1, NZ):
        to = (z + d) % NZ
        across.append(
            pltpu.make_async_remote_copy(
                src_ref=vs2.at[to // 2],
                dst_ref=vr2.at[d],
                send_sem=z_send.at[d],
                recv_sem=z_recv.at[d],
                device_id={"src": y * NZ + to, "tgt": t},
                device_id_type=MESH,
            )
        )
    for copy in across:
        copy.start()
    for copy in rows:
        copy.wait_recv()
    tiles = rr[...]
    labels = jnp.broadcast_to(rr[:, 0:1, 32:33], (2 * NT, 8, RAD))
    table = jnp.concatenate(
        [jnp.sum(jnp.where(labels == b + 1.0, tiles, 0.0), axis=0) for b in range(9)]
        + [jnp.zeros((8, RAD), F32)],
        axis=0,
    )
    listed[...] = table
    angles = lax.broadcasted_iota(jnp.int32, (80, NT * ANG), 1).astype(F32)
    onehot[...] = jnp.where(angles == table[:, 34:35], 1.0, 0.0).astype(BF16)
    vr2[0] = vs2[z // 2]
    for copy in across:
        copy.wait_recv()
    pair = vr2[0]
    for d in range(1, NZ):
        pair = pair + vr2[d]
    odd = (z % 2).astype(F32)
    own = pair * (1.0 - odd) + pltpu.roll(pair, 64, 1) * odd
    wall_ref[...] = own[0:3, 0:ANG]
    edge[...] = own
    walls[t] = own
    spread = [
        pltpu.make_async_remote_copy(
            src_ref=edge,
            dst_ref=walls.at[t],
            send_sem=e_send.at[k],
            recv_sem=e_recv.at[back(k)],
            device_id={"src": s, "tgt": peer(t, k)},
            device_id_type=MESH,
        )
        for k in range(1, NT)
    ]
    for copy in spread:
        copy.start()
    for copy in spread:
        copy.wait_recv()
    lane4 = lax.broadcasted_iota(jnp.int32, (4, 128), 1)
    before = pltpu.roll(walls[left], 72, 1)
    after = pltpu.roll(walls[right], 72, 1)
    ghosts = jnp.where(lane4 < 8, before, jnp.where(lane4 < 72, pltpu.roll(own, 8, 1), after))
    ghosts = jnp.where(lane4 < 80, ghosts, 0.0)
    upright = jnp.concatenate([ghosts, jnp.zeros((124, 128), F32)], axis=0).T

    ghost = [jnp.broadcast_to(upright[0:80, m : m + 1], (80, RAD)) for m in range(3)]
    w = advance([ext[0], ext[1], ext[2]], 2, ext[3], ext[4], ghost, True)
    for m in range(3):
        field_ref[m] = w[m][8:72]

    wide = [
        jnp.where(lane4 < ANG, walls[2 * n], pltpu.roll(walls[2 * n + 1], ANG, 1))
        for n in range(NT // 2)
    ]
    high, middle, low = split(jnp.concatenate(wide, axis=1))
    pieces = jnp.concatenate([high, middle, low, jnp.zeros_like(high)], axis=0).astype(BF16)
    found = lax.dot_general(
        onehot[...], pieces, (((1,), (1,)), ((), ())), preferred_element_type=F32
    )
    found = found[:, 0:4] + found[:, 4:8] + found[:, 8:12]
    table = listed[...]
    which = lax.broadcasted_iota(jnp.int32, (80, 4), 1).astype(F32) == table[:, 33:34]
    ghost = [
        jnp.broadcast_to(
            jnp.sum(jnp.where(which, found, 0.0), axis=1, keepdims=True), (80, RAD)
        ),
        jnp.broadcast_to(found[:, 2:3], (80, RAD)),
    ]
    shifted = [table] + [pltpu.roll(table, RAD - 8 * n, 1) for n in range(1, 4)]
    near = advance(shifted[0:2], 1, shifted[2], shifted[3], ghost, False)[0]
    lane1 = lax.broadcasted_iota(jnp.int32, (1, RAD), 1)
    for b in range(9):
        row = jnp.where(
            lane1 < SUBSTEPS, near[8 * b + 3 : 8 * b + 4], table[8 * b + 7 : 8 * b + 8]
        )
        there = jnp.broadcast_to(table[8 * b : 8 * b + 1, 32:33], (1, RAD)) > 0.0
        place = slice((b % 3) * RAD, (b % 3 + 1) * RAD)
        old = strength_ref[b // 3 : b // 3 + 1, place]
        new_ref[b // 3 : b // 3 + 1, place] = jnp.where(there, row, old)

    for copy in gather + halo + across + spread + rows:
        copy.wait_send()
    for g in range(NY - 1):
        to_y(g).wait_send()


def on_device(
    particle_position,
    particle_strength,
    core_radius,
    boundary_points,
    vorticity,
    swirl,
    diffusivity,
    intersection_source,
    intersection_target,
):
    prefactor = 1.6 / (4.0 * math.pi * math.sqrt(PART * NT * NY * NZ))
    vmem = pl.BlockSpec(memory_space=pltpu.VMEM)
    smem = pl.BlockSpec(memory_space=pltpu.SMEM)
    hbm = pl.BlockSpec(memory_space=pltpu.HBM)
    dma = pltpu.SemaphoreType.DMA
    wall, field, new = pl.pallas_call(
        lambda *refs: kernel(prefactor, *refs),
        out_shape=(
            jax.ShapeDtypeStruct((3, ANG), F32),
            jax.ShapeDtypeStruct((3, ANG, RAD), F32),
            jax.ShapeDtypeStruct((3, PART), F32),
        ),
        in_specs=[smem] * 2 + [hbm] * 7,
        out_specs=(vmem, vmem, vmem),
        scratch_shapes=[
            pltpu.VMEM((3, PART), F32),
            pltpu.VMEM((3, PART), F32),
            pltpu.VMEM((1, PART), F32),
            pltpu.VMEM((3, NY * NZ, ANG), F32),
            pltpu.VMEM((8, COLS), F32),
            pltpu.SMEM((4 * NT,), jnp.int32),
            pltpu.VMEM((NT, 8, PART), F32),
            pltpu.VMEM((64, COLS), BF16),
            pltpu.VMEM((NT * PART, 64), BF16),
            pltpu.VMEM((16, NT * PART), BF16),
            pltpu.VMEM((16, COLS), F32),
            pltpu.VMEM((5, 80, RAD), F32),
            pltpu.VMEM((NY, TILES, 4, 128), F32),
            pltpu.VMEM((NY - 1, TILES, 4, 128), F32),
            pltpu.VMEM((TILES, 4, 128), F32),
            pltpu.VMEM((NZ, 4, 128), F32),
            pltpu.VMEM((4, 128), F32),
            pltpu.VMEM((NT, 4, 128), F32),
            pltpu.VMEM((80, RAD), F32),
            pltpu.VMEM((80, NT * ANG), BF16),
            pltpu.VMEM((3 * ANG, RAD), F32),
            pltpu.VMEM((2 * NT, 8, RAD), F32),
            pltpu.VMEM((2 * NT, 8, RAD), F32),
            dma((NT,)),
            dma((NT,)),
            dma((7,)),
            dma((6,)),
            dma((6,)),
            dma((NY - 1,)),
            dma((NY - 1,)),
            dma((NZ,)),
            dma((NZ,)),
            dma((NT,)),
            dma((NT,)),
            dma((NT,)),
            dma((NT,)),
        ],
        compiler_params=pltpu.CompilerParams(
            collective_id=0, has_side_effects=True, vmem_limit_bytes=67_000_000
        ),
        name="wake",
    )(
        intersection_target.reshape(-1),
        intersection_source.reshape(-1),
        particle_position,
        particle_strength,
        core_radius,
        boundary_points,
        vorticity.reshape(3, ANG, RAD),
        swirl.reshape(ANG, RAD),
        diffusivity.reshape(ANG, RAD),
    )
    return (wall.reshape(3, 1, ANG), field.reshape(1, 3, ANG, RAD), new)


def solution(mesh):
    in_specs = (
        P(None, ("src", "tgt")),
        P(None, ("src", "tgt")),
        P(None, ("src", "tgt")),
        P(None, None, "tgt"),
        P("src", None, "tgt", None),
        P("src", "tgt", None),
        P("src", "tgt", None),
        P("src", "tgt", None),
        P("src", "tgt", None),
    )
    out_specs = (P(None, "src", "tgt"), P("src", None, "tgt", None), P(None, ("src", "tgt")))
    return jax.shard_map(
        on_device, mesh=mesh, in_specs=in_specs, out_specs=out_specs, check_vma=False
    )
```

```python
import math

import jax
import jax.numpy as jnp
from jax import lax
from jax.experimental import pallas as pl
from jax.experimental.pallas import tpu as pltpu
from jax.sharding import PartitionSpec as P

SUBSTEPS = 3
SWIRL_GAIN = 0.2
MESH = pl.DeviceIdType.MESH
F32 = jnp.float32
BF16 = jnp.bfloat16

NY, NZ = 4, 12
NX = 4
NT = 16
PART = 384
ANG = 64
RAD = 128
COLS = NY * NZ * ANG
PAIRS = NZ // 2
GROUP = NY * 128
HALF = COLS // 2
BATCH = 1024
GRAY = (0, 1, 3, 2)
BACK = (0, 2, 1, 3)


def peer(t, k):
    h, j, c = k // 8, (k // 2) % 4, k % 2
    x, hi, core = t // 4, (t // 2) % 2, t % 2
    return ((x + GRAY[j]) % NX) * 4 + ((hi + h) % 2) * 2 + (core + c) % 2


def back(k):
    return (k // 8) * 8 + BACK[(k // 2) % 4] * 2 + k % 2


def split(value):
    high = value.astype(BF16).astype(F32)
    rest = value - high
    middle = rest.astype(BF16).astype(F32)
    return high, middle, rest - middle


def advance(w, carrier, local_swirl, local_diff, ghost, closed):
    lane = lax.broadcasted_iota(jnp.int32, w[0].shape, 1)
    for _ in range(SUBSTEPS):
        half = 0.5 * (local_swirl + SWIRL_GAIN * w[carrier])
        moved = []
        for value, wall in zip(w, ghost):
            east = pltpu.roll(value, value.shape[0] - 1, 0)
            west = pltpu.roll(value, 1, 0)
            outward = pltpu.roll(value, RAD - 1, 1)
            if closed:
                outward = jnp.where(lane == RAD - 1, 0.0, outward)
            inward = jnp.where(lane == 0, wall, pltpu.roll(value, 1, 1))
            moved.append(
                value
                + local_diff * (east + west + outward + inward - 4.0 * value)
                - half * (east - west)
            )
        w = moved
    return w


def kernel(
    prefactor,
    codes_ref,
    sources_ref,
    position_ref,
    force_ref,
    radius_ref,
    points_ref,
    vort_ref,
    swirl_ref,
    diff_ref,
    wall_ref,
    field_ref,
    new_ref,
    pos,
    strength_ref,
    radius,
    points_in,
    x_ref,
    pick,
    chunk,
    tmat,
    pmat,
    fmat,
    acc,
    ext,
    vst,
    vr1,
    vs2,
    vr2,
    edge,
    walls,
    listed,
    onehot,
    fin,
    rs,
    rr,
    g_send,
    g_recv,
    loc,
    h_send,
    h_recv,
    y_send,
    y_recv,
    z_send,
    z_recv,
    e_send,
    e_recv,
    r_send,
    r_recv,
):
    s = lax.axis_index("src")
    t = lax.axis_index("tgt")
    y, z = s // NZ, s % NZ
    left, right = (t + NT - 1) % NT, (t + 1) % NT
    loads = [
        pltpu.make_async_copy(points_ref, points_in, loc.at[3]),
        pltpu.make_async_copy(position_ref, pos, loc.at[4]),
        pltpu.make_async_copy(force_ref, strength_ref, loc.at[5]),
        pltpu.make_async_copy(radius_ref, radius, loc.at[6]),
    ]
    for copy in loads:
        copy.start()

    friends = [{"src": s, "tgt": peer(t, k)} for k in range(1, NT)]
    friends += [{"src": ((y + d) % NY) * NZ + z, "tgt": t} for d in range(1, NY)]
    friends += [{"src": y * NZ + (z + d) % NZ, "tgt": t} for d in range(1, NZ)]
    barrier = pltpu.get_barrier_semaphore()

    for friend in friends:
        pl.semaphore_signal(barrier, inc=1, device_id=friend, device_id_type=MESH)

    inner = [
        pltpu.make_async_copy(vort_ref, ext.at[0:3, 8:72], loc.at[0]),
        pltpu.make_async_copy(swirl_ref, ext.at[3, 8:72], loc.at[1]),
        pltpu.make_async_copy(diff_ref, ext.at[4, 8:72], loc.at[2]),
    ]
    for copy in inner:
        copy.start()

    gather = [
        pltpu.make_async_remote_copy(
            src_ref=chunk.at[0],
            dst_ref=chunk.at[back(k)],
            send_sem=g_send.at[k],
            recv_sem=g_recv.at[back(k)],
            device_id={"src": s, "tgt": peer(t, k)},
            device_id_type=MESH,
        )
        for k in range(1, NT)
    ]
    halo = []
    for side, (to, rows, where) in enumerate(((right, 56, 0), (left, 0, 72))):
        for n, (src, dst) in enumerate(
            (
                (vort_ref.at[:, rows : rows + 8], ext.at[0:3, where : where + 8]),
                (swirl_ref.at[rows : rows + 8], ext.at[3, where : where + 8]),
                (diff_ref.at[rows : rows + 8], ext.at[4, where : where + 8]),
            )
        ):
            halo.append(
                pltpu.make_async_remote_copy(
                    src_ref=src,
                    dst_ref=dst,
                    send_sem=h_send.at[side * 3 + n],
                    recv_sem=h_recv.at[side * 3 + n],
                    device_id={"src": s, "tgt": to},
                    device_id_type=MESH,
                )
            )

    codes = [codes_ref[i] for i in range(9)]
    owners = [jnp.where(code >= 0, code // 9, -1) for code in codes]
    slots = []
    for i in range(9):
        rank = jnp.int32(0)
        for j in range(i):
            rank = rank + jnp.where(owners[j] == owners[i], 1, 0)
        slots.append(jnp.where(codes[i] >= 0, owners[i] * 2 + rank, -1))
    for k in range(NT):
        for n in range(2):
            row, name = jnp.int32(0), jnp.int32(0)
            for i in range(9):
                here = slots[i] == 2 * peer(t, k) + n
                row = jnp.where(here, sources_ref[i], row)
                name = jnp.where(here, codes[i] % 9 + 1, name)
            pick[2 * k + n] = row
            pick[2 * NT + 2 * k + n] = name

    loads[0].wait()
    pairs = []
    for m in range(3):
        even = points_in[m, pl.ds(0, NY * NZ // 2, stride=2), :]
        odd_ones = points_in[m, pl.ds(1, NY * NZ // 2, stride=2), :]
        pairs.append(jnp.concatenate([even, odd_ones], axis=1) - 0.5)
    square = pairs[0] * pairs[0] + pairs[1] * pairs[1] + pairs[2] * pairs[2]
    for q in range(COLS // 128):
        at = (q % PAIRS * NY + q // PAIRS) * 128
        x_ref[:, at : at + 128] = jnp.concatenate(
            [pairs[m][q : q + 1] for m in range(3)]
            + [jnp.ones((1, 128), F32), jnp.zeros((3, 128), F32), square[q : q + 1]],
            axis=0,
        )
    high, middle, low = split(x_ref[...])
    none = jnp.zeros_like(high)
    tmat[...] = jnp.concatenate([high, middle, low, high, middle, high, none, none], axis=0).astype(
        BF16
    )
    acc[...] = jnp.zeros_like(acc)
    for copy in loads[1:]:
        copy.wait()
    centred = [pos[m : m + 1] - 0.5 for m in range(3)]
    core = radius[...]
    chunk[0] = jnp.concatenate(
        [-2.0 * c for c in centred]
        + [
            centred[0] * centred[0]
            + centred[1] * centred[1]
            + centred[2] * centred[2]
            + core * core
        ]
        + [strength_ref[m : m + 1] for m in range(3)]
        + [jnp.zeros((1, PART), F32)],
        axis=0,
    )

    def factor(block, p_out, f_out):
        size = block.shape[1]
        row = lax.broadcasted_iota(jnp.int32, block.shape, 0)
        high, middle, low = split(jnp.where(row == 7, 1.0, block))
        none = jnp.zeros_like(high)
        stacked = jnp.concatenate([high, high, high, middle, middle, low, none, none], axis=0)
        p_out[...] = stacked.T.astype(BF16)
        p = [-0.5 * block[n : n + 1] for n in range(3)]
        q = [block[n : n + 1] for n in range(4, 7)]
        moment = [
            q[1] * p[2] - q[2] * p[1],
            q[2] * p[0] - q[0] * p[2],
            q[0] * p[1] - q[1] * p[0],
        ]
        factors = jnp.concatenate(q + moment + [jnp.zeros((2, size), F32)], axis=0)
        coarse = factors.astype(BF16).astype(F32)
        f_out[...] = jnp.concatenate([coarse, factors - coarse], axis=0).astype(BF16)

    def span(n):
        return pl.ds(pl.multiple_of(n * PART, PART), PART)

    def prepare(n):
        factor(chunk[n], pmat.at[span(n)], fmat.at[:, span(n)])

    def absorb(total, p, factors, points):
        squared = jnp.dot(p, points, preferred_element_type=F32)
        weight = lax.rsqrt(squared * squared * squared)
        coarse = weight.astype(BF16)
        fine = (weight - coarse.astype(F32)).astype(BF16)
        return (
            total
            + jnp.dot(factors, coarse, preferred_element_type=F32)
            + jnp.dot(factors, fine, preferred_element_type=F32)
        )

    def absorb_all(p, factors):
        for part in range(2):
            cols = slice(part * HALF, (part + 1) * HALF)
            acc[:, cols] = absorb(acc[:, cols], p, factors, tmat[:, cols])

    factor(chunk[0], pmat.at[0:PART], fmat.at[:, 0:PART])
    absorb_all(pmat[0:PART, :], fmat[:, 0:PART])

    pl.semaphore_wait(barrier, len(friends))
    for copy in gather:
        copy.start()
    for copy in halo:
        copy.start()

    def first(n, carry):
        pltpu.make_async_copy(chunk.at[0], chunk.at[n], g_recv.at[n]).wait()
        prepare(n)
        absorb_all(pmat[span(n), :], fmat[:, span(n)])
        return carry

    lax.fori_loop(1, NT // 2, first, 0)

    for copy in inner:
        copy.wait()
    for copy in halo:
        copy.wait_recv()
    nothing = jnp.zeros((80, RAD), F32)
    w = advance([ext[0], ext[1], ext[2]], 2, ext[3], ext[4], [nothing] * 3, True)
    for m in range(3):
        fin[m * ANG : (m + 1) * ANG] = w[m][8:72]
    lane8 = lax.broadcasted_iota(jnp.int32, (8, RAD), 1)
    row8 = lax.broadcasted_iota(jnp.int32, (8, RAD), 0)

    def gather_row(n, carry):
        block = pick[n]
        m, a = block // ANG, block % ANG
        rows = pl.ds(a + 5, 8)
        tile = jnp.where(
            lane8 < 8,
            ext[m, rows, :],
            jnp.where(
                lane8 < 16,
                pltpu.roll(ext[2, rows, :], 8, 1),
                jnp.where(
                    lane8 < 24,
                    pltpu.roll(ext[3, rows, :], 16, 1),
                    pltpu.roll(ext[4, rows, :], 24, 1),
                ),
            ),
        )
        angle = (row8 + (t * ANG + a + NT * ANG - 3)) % (NT * ANG)
        tile = jnp.where(lane8 == 32, pick[2 * NT + n].astype(F32), tile)
        tile = jnp.where(lane8 == 33, m.astype(F32), tile)
        tile = jnp.where(lane8 == 34, angle.astype(F32), tile)
        rs[n] = jnp.where(row8 == 7, fin[pl.ds(block, 1), :], tile)
        return carry

    lax.fori_loop(0, 2 * NT, gather_row, 0)
    rr[0:2] = rs[0:2]
    rows = [
        pltpu.make_async_remote_copy(
            src_ref=rs.at[2 * k : 2 * k + 2],
            dst_ref=rr.at[2 * back(k) : 2 * back(k) + 2],
            send_sem=r_send.at[k],
            recv_sem=r_recv.at[back(k)],
            device_id={"src": s, "tgt": peer(t, k)},
            device_id_type=MESH,
        )
        for k in range(1, NT)
    ]
    for copy in rows:
        copy.start()

    def second(n, carry):
        pltpu.make_async_copy(chunk.at[0], chunk.at[n], g_recv.at[n]).wait()
        prepare(n)
        return carry

    lax.fori_loop(NT // 2, NT, second, 0)

    def pair_of(g):
        return (z // 2 + 3 + (g + 1) // 2 * (1 - 2 * (g % 2))) % PAIRS

    def to_z(g, n, plane):
        return pltpu.make_async_remote_copy(
            src_ref=vst.at[g],
            dst_ref=vr1.at[z],
            send_sem=z_send.at[2 * g + n],
            recv_sem=z_recv.at[z],
            device_id={"src": y * NZ + plane, "tgt": t},
            device_id_type=MESH,
        )

    partner = z + 1 - 2 * (z % 2)

    def plane_group(g, carry):
        q = pair_of(g)
        cols = pl.ds(pl.multiple_of(q * GROUP, GROUP), GROUP)
        points = tmat[:, cols]

        def step(n, total):
            where = pl.ds(pl.multiple_of(n * BATCH, BATCH), BATCH)
            return absorb(total, pmat[where, :], fmat[:, where], points)

        batches = NT * PART // BATCH
        total = lax.fori_loop(batches // 2, batches, step, acc[:, cols])
        both = total[0:8] + total[8:16]
        place = x_ref[:, cols]
        x = [place[n : n + 1] for n in range(3)]
        q3 = [both[n : n + 1] for n in range(3)]
        velocity = jnp.concatenate(
            [
                q3[1] * x[2] - q3[2] * x[1] - both[3:4],
                q3[2] * x[0] - q3[0] * x[2] - both[4:5],
                q3[0] * x[1] - q3[1] * x[0] - both[5:6],
                jnp.zeros((1, GROUP), F32),
            ],
            axis=0,
        )
        velocity = velocity * prefactor
        for n in range(NY):
            vst[g, n] = velocity[:, n * 128 : (n + 1) * 128]

        @pl.when(g < PAIRS - 1)
        def _():
            for n in range(2):
                to_z(g, n, 2 * q + n).start()

        return carry

    lax.fori_loop(0, PAIRS, plane_group, 0)
    to_z(PAIRS - 1, 0, partner).start()
    for copy in rows:
        copy.wait_recv()
    tiles = rr[...]
    labels = jnp.broadcast_to(rr[:, 0:1, 32:33], (2 * NT, 8, RAD))
    table = jnp.concatenate(
        [jnp.sum(jnp.where(labels == b + 1.0, tiles, 0.0), axis=0) for b in range(9)]
        + [jnp.zeros((8, RAD), F32)],
        axis=0,
    )
    listed[...] = table
    angles = lax.broadcasted_iota(jnp.int32, (80, NT * ANG), 1).astype(F32)
    onehot[...] = jnp.where(angles == table[:, 34:35], 1.0, 0.0).astype(BF16)
    summed = vst[PAIRS - 1]
    for d in range(1, NZ):
        other = (z + d) % NZ
        pltpu.make_async_copy(vst.at[0], vr1.at[other], z_recv.at[other]).wait()
        summed = summed + vr1[other]
    vs2[...] = summed
    across = [
        pltpu.make_async_remote_copy(
            src_ref=vs2.at[(y + d) % NY],
            dst_ref=vr2.at[d],
            send_sem=y_send.at[d],
            recv_sem=y_recv.at[d],
            device_id={"src": (y + d) % NY * NZ + z, "tgt": t},
            device_id_type=MESH,
        )
        for d in range(1, NY)
    ]
    for copy in across:
        copy.start()
    for copy in across:
        copy.wait_recv()
    pair = vs2[y] + vr2[1] + vr2[2] + vr2[3]
    odd = (z % 2).astype(F32)
    own = pair * (1.0 - odd) + pltpu.roll(pair, 64, 1) * odd
    wall_ref[...] = own[0:3, 0:ANG]
    edge[...] = own
    walls[t] = own
    spread = [
        pltpu.make_async_remote_copy(
            src_ref=edge,
            dst_ref=walls.at[t],
            send_sem=e_send.at[k],
            recv_sem=e_recv.at[back(k)],
            device_id={"src": s, "tgt": peer(t, k)},
            device_id_type=MESH,
        )
        for k in range(1, NT)
    ]
    for copy in spread:
        copy.start()
    for copy in spread:
        copy.wait_recv()
    lane4 = lax.broadcasted_iota(jnp.int32, (4, 128), 1)
    before = pltpu.roll(walls[left], 72, 1)
    after = pltpu.roll(walls[right], 72, 1)
    ghosts = jnp.where(lane4 < 8, before, jnp.where(lane4 < 72, pltpu.roll(own, 8, 1), after))
    ghosts = jnp.where(lane4 < 80, ghosts, 0.0)
    upright = jnp.concatenate([ghosts, jnp.zeros((124, 128), F32)], axis=0).T

    ghost = [jnp.broadcast_to(upright[0:80, m : m + 1], (80, RAD)) for m in range(3)]
    w = advance([ext[0], ext[1], ext[2]], 2, ext[3], ext[4], ghost, True)
    for m in range(3):
        field_ref[m] = w[m][8:72]

    wide = [
        jnp.where(lane4 < ANG, walls[2 * n], pltpu.roll(walls[2 * n + 1], ANG, 1))
        for n in range(NT // 2)
    ]
    high, middle, low = split(jnp.concatenate(wide, axis=1))
    pieces = jnp.concatenate([high, middle, low, jnp.zeros_like(high)], axis=0).astype(BF16)
    found = lax.dot_general(
        onehot[...], pieces, (((1,), (1,)), ((), ())), preferred_element_type=F32
    )
    found = found[:, 0:4] + found[:, 4:8] + found[:, 8:12]
    table = listed[...]
    which = lax.broadcasted_iota(jnp.int32, (80, 4), 1).astype(F32) == table[:, 33:34]
    ghost = [
        jnp.broadcast_to(
            jnp.sum(jnp.where(which, found, 0.0), axis=1, keepdims=True), (80, RAD)
        ),
        jnp.broadcast_to(found[:, 2:3], (80, RAD)),
    ]
    shifted = [table] + [pltpu.roll(table, RAD - 8 * n, 1) for n in range(1, 4)]
    near = advance(shifted[0:2], 1, shifted[2], shifted[3], ghost, False)[0]
    lane1 = lax.broadcasted_iota(jnp.int32, (1, RAD), 1)
    for b in range(9):
        row = jnp.where(
            lane1 < SUBSTEPS, near[8 * b + 3 : 8 * b + 4], table[8 * b + 7 : 8 * b + 8]
        )
        there = jnp.broadcast_to(table[8 * b : 8 * b + 1, 32:33], (1, RAD)) > 0.0
        place = slice((b % 3) * RAD, (b % 3 + 1) * RAD)
        old = strength_ref[b // 3 : b // 3 + 1, place]
        new_ref[b // 3 : b // 3 + 1, place] = jnp.where(there, row, old)

    for copy in gather + halo + across + spread + rows:
        copy.wait_send()
    for g in range(PAIRS - 1):
        for n in range(2):
            to_z(g, n, partner).wait_send()
    to_z(PAIRS - 1, 0, partner).wait_send()


def hand_over(wall_ref, field_ref, new_ref, wall_out, field_out, new_out):
    wall_out[:, 0] = wall_ref[...]
    field_out[0] = field_ref[...]
    new_out[...] = new_ref[...]


def on_device(
    particle_position,
    particle_strength,
    core_radius,
    boundary_points,
    vorticity,
    swirl,
    diffusivity,
    intersection_source,
    intersection_target,
):
    prefactor = 1.6 / (4.0 * math.pi * math.sqrt(PART * NT * NY * NZ))
    vmem = pl.BlockSpec(memory_space=pltpu.VMEM)
    smem = pl.BlockSpec(memory_space=pltpu.SMEM)
    hbm = pl.BlockSpec(memory_space=pltpu.HBM)
    dma = pltpu.SemaphoreType.DMA
    wall, field, new = pl.pallas_call(
        lambda *refs: kernel(prefactor, *refs),
        out_shape=(
            jax.ShapeDtypeStruct((3, ANG), F32),
            jax.ShapeDtypeStruct((3, ANG, RAD), F32),
            jax.ShapeDtypeStruct((3, PART), F32),
        ),
        in_specs=[smem] * 2 + [hbm] * 7,
        out_specs=(vmem, vmem, vmem),
        scratch_shapes=[
            pltpu.VMEM((3, PART), F32),
            pltpu.VMEM((3, PART), F32),
            pltpu.VMEM((1, PART), F32),
            pltpu.VMEM((3, NY * NZ, ANG), F32),
            pltpu.VMEM((8, COLS), F32),
            pltpu.SMEM((4 * NT,), jnp.int32),
            pltpu.VMEM((NT, 8, PART), F32),
            pltpu.VMEM((64, COLS), BF16),
            pltpu.VMEM((NT * PART, 64), BF16),
            pltpu.VMEM((16, NT * PART), BF16),
            pltpu.VMEM((16, COLS), F32),
            pltpu.VMEM((5, 80, RAD), F32),
            pltpu.VMEM((PAIRS, NY, 4, 128), F32),
            pltpu.VMEM((NZ, NY, 4, 128), F32),
            pltpu.VMEM((NY, 4, 128), F32),
            pltpu.VMEM((NY, 4, 128), F32),
            pltpu.VMEM((4, 128), F32),
            pltpu.VMEM((NT, 4, 128), F32),
            pltpu.VMEM((80, RAD), F32),
            pltpu.VMEM((80, NT * ANG), BF16),
            pltpu.VMEM((3 * ANG, RAD), F32),
            pltpu.VMEM((2 * NT, 8, RAD), F32),
            pltpu.VMEM((2 * NT, 8, RAD), F32),
            dma((NT,)),
            dma((NT,)),
            dma((7,)),
            dma((6,)),
            dma((6,)),
            dma((NY,)),
            dma((NY,)),
            dma((NZ,)),
            dma((NZ,)),
            dma((NT,)),
            dma((NT,)),
            dma((NT,)),
            dma((NT,)),
        ],
        compiler_params=pltpu.CompilerParams(
            collective_id=0, has_side_effects=True, vmem_limit_bytes=67_000_000
        ),
        name="wake",
    )(
        intersection_target.reshape(-1),
        intersection_source.reshape(-1),
        particle_position,
        particle_strength,
        core_radius,
        boundary_points,
        vorticity.reshape(3, ANG, RAD),
        swirl.reshape(ANG, RAD),
        diffusivity.reshape(ANG, RAD),
    )
    return pl.pallas_call(
        hand_over,
        out_shape=(
            jax.ShapeDtypeStruct((3, 1, ANG), F32),
            jax.ShapeDtypeStruct((1, 3, ANG, RAD), F32),
            jax.ShapeDtypeStruct((3, PART), F32),
        ),
        in_specs=[vmem] * 3,
        out_specs=(vmem,) * 3,
        name="hand_over",
        compiler_params=pltpu.CompilerParams(vmem_limit_bytes=67_000_000),
    )(wall, field, new)


def solution(mesh):
    in_specs = (
        P(None, ("src", "tgt")),
        P(None, ("src", "tgt")),
        P(None, ("src", "tgt")),
        P(None, None, "tgt"),
        P("src", None, "tgt", None),
        P("src", "tgt", None),
        P("src", "tgt", None),
        P("src", "tgt", None),
        P("src", "tgt", None),
    )
    out_specs = (P(None, "src", "tgt"), P("src", None, "tgt", None), P(None, ("src", "tgt")))
    return jax.shard_map(
        on_device, mesh=mesh, in_specs=in_specs, out_specs=out_specs, check_vma=False
    )
```

```python
import math

import jax
import jax.numpy as jnp
from jax import lax
from jax.experimental import pallas as pl
from jax.experimental.pallas import tpu as pltpu
from jax.sharding import PartitionSpec as P

SUBSTEPS = 3
SWIRL_GAIN = 0.2
MESH = pl.DeviceIdType.MESH
F32 = jnp.float32
BF16 = jnp.bfloat16

NY, NZ = 4, 12
NX = 4
NT = 16
PART = 384
ANG = 64
RAD = 128
COLS = NY * NZ * ANG
PAIRS = NZ // 2
GROUP = NY * 128
HALF = COLS // 2
BATCH = 1024
GRAY = (0, 1, 3, 2)
BACK = (0, 2, 1, 3)


def peer(t, k):
    h, j, c = k // 8, (k // 2) % 4, k % 2
    x, hi, core = t // 4, (t // 2) % 2, t % 2
    return ((x + GRAY[j]) % NX) * 4 + ((hi + h) % 2) * 2 + (core + c) % 2


def back(k):
    return (k // 8) * 8 + BACK[(k // 2) % 4] * 2 + k % 2


def split(value):
    high = value.astype(BF16).astype(F32)
    rest = value - high
    middle = rest.astype(BF16).astype(F32)
    return high, middle, rest - middle


def advance(w, carrier, local_swirl, local_diff, ghost, closed):
    lane = lax.broadcasted_iota(jnp.int32, w[0].shape, 1)
    for _ in range(SUBSTEPS):
        half = 0.5 * (local_swirl + SWIRL_GAIN * w[carrier])
        moved = []
        for value, wall in zip(w, ghost):
            east = pltpu.roll(value, value.shape[0] - 1, 0)
            west = pltpu.roll(value, 1, 0)
            outward = pltpu.roll(value, RAD - 1, 1)
            if closed:
                outward = jnp.where(lane == RAD - 1, 0.0, outward)
            inward = jnp.where(lane == 0, wall, pltpu.roll(value, 1, 1))
            moved.append(
                value
                + local_diff * (east + west + outward + inward - 4.0 * value)
                - half * (east - west)
            )
        w = moved
    return w


def kernel(
    prefactor,
    codes_ref,
    sources_ref,
    position_ref,
    force_ref,
    radius_ref,
    points_ref,
    vort_ref,
    swirl_ref,
    diff_ref,
    wall_ref,
    field_ref,
    new_ref,
    pos,
    strength_ref,
    radius,
    points_in,
    x_ref,
    pick,
    chunk,
    tmat,
    pmat,
    fmat,
    acc,
    ext,
    vst,
    vr1,
    vs2,
    vr2,
    edge,
    walls,
    listed,
    onehot,
    fin,
    rs,
    rr,
    g_send,
    g_recv,
    loc,
    h_send,
    h_recv,
    y_send,
    y_recv,
    z_send,
    z_recv,
    e_send,
    e_recv,
    r_send,
    r_recv,
):
    s = lax.axis_index("src")
    t = lax.axis_index("tgt")
    y, z = s // NZ, s % NZ
    left, right = (t + NT - 1) % NT, (t + 1) % NT
    loads = [
        pltpu.make_async_copy(points_ref, points_in, loc.at[3]),
        pltpu.make_async_copy(position_ref, pos, loc.at[4]),
        pltpu.make_async_copy(force_ref, strength_ref, loc.at[5]),
        pltpu.make_async_copy(radius_ref, radius, loc.at[6]),
    ]
    for copy in loads:
        copy.start()

    friends = [{"src": s, "tgt": peer(t, k)} for k in range(1, NT)]
    friends += [{"src": ((y + d) % NY) * NZ + z, "tgt": t} for d in range(1, NY)]
    friends += [{"src": y * NZ + (z + d) % NZ, "tgt": t} for d in range(1, NZ)]
    barrier = pltpu.get_barrier_semaphore()

    for friend in friends:
        pl.semaphore_signal(barrier, inc=1, device_id=friend, device_id_type=MESH)

    inner = [
        pltpu.make_async_copy(vort_ref, ext.at[0:3, 8:72], loc.at[0]),
        pltpu.make_async_copy(swirl_ref, ext.at[3, 8:72], loc.at[1]),
        pltpu.make_async_copy(diff_ref, ext.at[4, 8:72], loc.at[2]),
    ]
    for copy in inner:
        copy.start()

    gather = [
        pltpu.make_async_remote_copy(
            src_ref=chunk.at[0],
            dst_ref=chunk.at[back(k)],
            send_sem=g_send.at[k],
            recv_sem=g_recv.at[back(k)],
            device_id={"src": s, "tgt": peer(t, k)},
            device_id_type=MESH,
        )
        for k in range(1, NT)
    ]
    halo = []
    for side, (to, rows, where) in enumerate(((right, 56, 0), (left, 0, 72))):
        for n, (src, dst) in enumerate(
            (
                (vort_ref.at[:, rows : rows + 8], ext.at[0:3, where : where + 8]),
                (swirl_ref.at[rows : rows + 8], ext.at[3, where : where + 8]),
                (diff_ref.at[rows : rows + 8], ext.at[4, where : where + 8]),
            )
        ):
            halo.append(
                pltpu.make_async_remote_copy(
                    src_ref=src,
                    dst_ref=dst,
                    send_sem=h_send.at[side * 3 + n],
                    recv_sem=h_recv.at[side * 3 + n],
                    device_id={"src": s, "tgt": to},
                    device_id_type=MESH,
                )
            )

    loads[0].wait()
    pairs = []
    for m in range(3):
        even = points_in[m, pl.ds(0, NY * NZ // 2, stride=2), :]
        odd_ones = points_in[m, pl.ds(1, NY * NZ // 2, stride=2), :]
        pairs.append(jnp.concatenate([even, odd_ones], axis=1) - 0.5)
    square = pairs[0] * pairs[0] + pairs[1] * pairs[1] + pairs[2] * pairs[2]
    for q in range(COLS // 128):
        at = (q % PAIRS * NY + q // PAIRS) * 128
        x_ref[:, at : at + 128] = jnp.concatenate(
            [pairs[m][q : q + 1] for m in range(3)]
            + [jnp.ones((1, 128), F32), jnp.zeros((3, 128), F32), square[q : q + 1]],
            axis=0,
        )
    high, middle, low = split(x_ref[...])
    none = jnp.zeros_like(high)
    tmat[...] = jnp.concatenate([high, middle, low, high, middle, high, none, none], axis=0).astype(
        BF16
    )
    acc[...] = jnp.zeros_like(acc)
    for copy in loads[1:]:
        copy.wait()
    centred = [pos[m : m + 1] - 0.5 for m in range(3)]
    core = radius[...]
    chunk[0] = jnp.concatenate(
        [-2.0 * c for c in centred]
        + [
            centred[0] * centred[0]
            + centred[1] * centred[1]
            + centred[2] * centred[2]
            + core * core
        ]
        + [strength_ref[m : m + 1] for m in range(3)]
        + [jnp.zeros((1, PART), F32)],
        axis=0,
    )

    def factor(block, p_out, f_out):
        size = block.shape[1]
        row = lax.broadcasted_iota(jnp.int32, block.shape, 0)
        high, middle, low = split(jnp.where(row == 7, 1.0, block))
        none = jnp.zeros_like(high)
        stacked = jnp.concatenate([high, high, high, middle, middle, low, none, none], axis=0)
        p_out[...] = stacked.T.astype(BF16)
        p = [-0.5 * block[n : n + 1] for n in range(3)]
        q = [block[n : n + 1] for n in range(4, 7)]
        moment = [
            q[1] * p[2] - q[2] * p[1],
            q[2] * p[0] - q[0] * p[2],
            q[0] * p[1] - q[1] * p[0],
        ]
        factors = jnp.concatenate(q + moment + [jnp.zeros((2, size), F32)], axis=0)
        coarse = factors.astype(BF16).astype(F32)
        f_out[...] = jnp.concatenate([coarse, factors - coarse], axis=0).astype(BF16)

    def span(n):
        return pl.ds(pl.multiple_of(n * PART, PART), PART)

    def prepare(n):
        factor(chunk[n], pmat.at[span(n)], fmat.at[:, span(n)])

    def absorb(total, p, factors, points):
        squared = jnp.dot(p, points, preferred_element_type=F32)
        weight = lax.rsqrt(squared * squared * squared)
        coarse = weight.astype(BF16)
        fine = (weight - coarse.astype(F32)).astype(BF16)
        return (
            total
            + jnp.dot(factors, coarse, preferred_element_type=F32)
            + jnp.dot(factors, fine, preferred_element_type=F32)
        )

    def absorb_all(p, factors):
        for part in range(2):
            cols = slice(part * HALF, (part + 1) * HALF)
            acc[:, cols] = absorb(acc[:, cols], p, factors, tmat[:, cols])

    factor(chunk[0], pmat.at[0:PART], fmat.at[:, 0:PART])
    absorb_all(pmat[0:PART, :], fmat[:, 0:PART])

    pl.semaphore_wait(barrier, len(friends))
    for copy in gather:
        copy.start()
    for copy in halo:
        copy.start()

    codes = [codes_ref[i] for i in range(9)]
    owners = [jnp.where(code >= 0, code // 9, -1) for code in codes]
    slots = []
    for i in range(9):
        rank = jnp.int32(0)
        for j in range(i):
            rank = rank + jnp.where(owners[j] == owners[i], 1, 0)
        slots.append(jnp.where(codes[i] >= 0, owners[i] * 2 + rank, -1))
    for k in range(NT):
        for n in range(2):
            row, name = jnp.int32(0), jnp.int32(0)
            for i in range(9):
                here = slots[i] == 2 * peer(t, k) + n
                row = jnp.where(here, sources_ref[i], row)
                name = jnp.where(here, codes[i] % 9 + 1, name)
            pick[2 * k + n] = row
            pick[2 * NT + 2 * k + n] = name

    def first(n, carry):
        pltpu.make_async_copy(chunk.at[0], chunk.at[n], g_recv.at[n]).wait()
        prepare(n)
        absorb_all(pmat[span(n), :], fmat[:, span(n)])
        return carry

    lax.fori_loop(1, NT // 2, first, 0)

    def second(n, carry):
        pltpu.make_async_copy(chunk.at[0], chunk.at[n], g_recv.at[n]).wait()
        prepare(n)
        return carry

    lax.fori_loop(NT // 2, NT, second, 0)

    def pair_of(g):
        return (z // 2 + 3 + (g + 1) // 2 * (1 - 2 * (g % 2))) % PAIRS

    def to_z(g, n, plane):
        return pltpu.make_async_remote_copy(
            src_ref=vst.at[g],
            dst_ref=vr1.at[z],
            send_sem=z_send.at[2 * g + n],
            recv_sem=z_recv.at[z],
            device_id={"src": y * NZ + plane, "tgt": t},
            device_id_type=MESH,
        )

    partner = z + 1 - 2 * (z % 2)

    def plane_group(g, carry):
        q = pair_of(g)
        cols = pl.ds(pl.multiple_of(q * GROUP, GROUP), GROUP)
        points = tmat[:, cols]

        def step(n, total):
            where = pl.ds(pl.multiple_of(n * BATCH, BATCH), BATCH)
            return absorb(total, pmat[where, :], fmat[:, where], points)

        batches = NT * PART // BATCH
        total = lax.fori_loop(batches // 2, batches, step, acc[:, cols])
        both = total[0:8] + total[8:16]
        place = x_ref[:, cols]
        x = [place[n : n + 1] for n in range(3)]
        q3 = [both[n : n + 1] for n in range(3)]
        velocity = jnp.concatenate(
            [
                q3[1] * x[2] - q3[2] * x[1] - both[3:4],
                q3[2] * x[0] - q3[0] * x[2] - both[4:5],
                q3[0] * x[1] - q3[1] * x[0] - both[5:6],
                jnp.zeros((1, GROUP), F32),
            ],
            axis=0,
        )
        velocity = velocity * prefactor
        for n in range(NY):
            vst[g, n] = velocity[:, n * 128 : (n + 1) * 128]

        @pl.when(g < PAIRS - 1)
        def _():
            for n in range(2):
                to_z(g, n, 2 * q + n).start()

        return carry

    lax.fori_loop(0, PAIRS, plane_group, 0)
    to_z(PAIRS - 1, 0, partner).start()

    for copy in inner:
        copy.wait()
    for copy in halo:
        copy.wait_recv()
    nothing = jnp.zeros((80, RAD), F32)
    w = advance([ext[0], ext[1], ext[2]], 2, ext[3], ext[4], [nothing] * 3, True)
    for m in range(3):
        fin[m * ANG : (m + 1) * ANG] = w[m][8:72]
    lane8 = lax.broadcasted_iota(jnp.int32, (8, RAD), 1)
    row8 = lax.broadcasted_iota(jnp.int32, (8, RAD), 0)

    def gather_row(n, carry):
        block = pick[n]
        m, a = block // ANG, block % ANG
        rows = pl.ds(a + 5, 8)
        tile = jnp.where(
            lane8 < 8,
            ext[m, rows, :],
            jnp.where(
                lane8 < 16,
                pltpu.roll(ext[2, rows, :], 8, 1),
                jnp.where(
                    lane8 < 24,
                    pltpu.roll(ext[3, rows, :], 16, 1),
                    pltpu.roll(ext[4, rows, :], 24, 1),
                ),
            ),
        )
        angle = (row8 + (t * ANG + a + NT * ANG - 3)) % (NT * ANG)
        tile = jnp.where(lane8 == 32, pick[2 * NT + n].astype(F32), tile)
        tile = jnp.where(lane8 == 33, m.astype(F32), tile)
        tile = jnp.where(lane8 == 34, angle.astype(F32), tile)
        rs[n] = jnp.where(row8 == 7, fin[pl.ds(block, 1), :], tile)
        return carry

    lax.fori_loop(0, 2 * NT, gather_row, 0)
    rr[0:2] = rs[0:2]
    rows = [
        pltpu.make_async_remote_copy(
            src_ref=rs.at[2 * k : 2 * k + 2],
            dst_ref=rr.at[2 * back(k) : 2 * back(k) + 2],
            send_sem=r_send.at[k],
            recv_sem=r_recv.at[back(k)],
            device_id={"src": s, "tgt": peer(t, k)},
            device_id_type=MESH,
        )
        for k in range(1, NT)
    ]
    for copy in rows:
        copy.start()

    summed = vst[PAIRS - 1]
    for d in range(1, NZ):
        other = (z + d) % NZ
        pltpu.make_async_copy(vst.at[0], vr1.at[other], z_recv.at[other]).wait()
        summed = summed + vr1[other]
    vs2[...] = summed
    across = [
        pltpu.make_async_remote_copy(
            src_ref=vs2.at[(y + d) % NY],
            dst_ref=vr2.at[d],
            send_sem=y_send.at[d],
            recv_sem=y_recv.at[d],
            device_id={"src": (y + d) % NY * NZ + z, "tgt": t},
            device_id_type=MESH,
        )
        for d in range(1, NY)
    ]
    for copy in across:
        copy.start()
    for copy in across:
        copy.wait_recv()
    pair = vs2[y] + vr2[1] + vr2[2] + vr2[3]
    odd = (z % 2).astype(F32)
    own = pair * (1.0 - odd) + pltpu.roll(pair, 64, 1) * odd
    wall_ref[...] = own[0:3, 0:ANG]
    edge[...] = own
    walls[t] = own
    spread = [
        pltpu.make_async_remote_copy(
            src_ref=edge,
            dst_ref=walls.at[t],
            send_sem=e_send.at[k],
            recv_sem=e_recv.at[back(k)],
            device_id={"src": s, "tgt": peer(t, k)},
            device_id_type=MESH,
        )
        for k in range(1, NT)
    ]
    for copy in spread:
        copy.start()
    for copy in rows:
        copy.wait_recv()
    tiles = rr[...]
    labels = jnp.broadcast_to(rr[:, 0:1, 32:33], (2 * NT, 8, RAD))
    table = jnp.concatenate(
        [jnp.sum(jnp.where(labels == b + 1.0, tiles, 0.0), axis=0) for b in range(9)]
        + [jnp.zeros((8, RAD), F32)],
        axis=0,
    )
    listed[...] = table
    angles = lax.broadcasted_iota(jnp.int32, (80, NT * ANG), 1).astype(F32)
    onehot[...] = jnp.where(angles == table[:, 34:35], 1.0, 0.0).astype(BF16)
    for copy in spread:
        copy.wait_recv()
    lane4 = lax.broadcasted_iota(jnp.int32, (4, 128), 1)
    before = pltpu.roll(walls[left], 72, 1)
    after = pltpu.roll(walls[right], 72, 1)
    ghosts = jnp.where(lane4 < 8, before, jnp.where(lane4 < 72, pltpu.roll(own, 8, 1), after))
    ghosts = jnp.where(lane4 < 80, ghosts, 0.0)
    upright = jnp.concatenate([ghosts, jnp.zeros((124, 128), F32)], axis=0).T

    ghost = [jnp.broadcast_to(upright[0:80, m : m + 1], (80, RAD)) for m in range(3)]
    w = advance([ext[0], ext[1], ext[2]], 2, ext[3], ext[4], ghost, True)
    for m in range(3):
        field_ref[m] = w[m][8:72]

    wide = [
        jnp.where(lane4 < ANG, walls[2 * n], pltpu.roll(walls[2 * n + 1], ANG, 1))
        for n in range(NT // 2)
    ]
    high, middle, low = split(jnp.concatenate(wide, axis=1))
    pieces = jnp.concatenate([high, middle, low, jnp.zeros_like(high)], axis=0).astype(BF16)
    found = lax.dot_general(
        onehot[...], pieces, (((1,), (1,)), ((), ())), preferred_element_type=F32
    )
    found = found[:, 0:4] + found[:, 4:8] + found[:, 8:12]
    table = listed[...]
    which = lax.broadcasted_iota(jnp.int32, (80, 4), 1).astype(F32) == table[:, 33:34]
    ghost = [
        jnp.broadcast_to(
            jnp.sum(jnp.where(which, found, 0.0), axis=1, keepdims=True), (80, RAD)
        ),
        jnp.broadcast_to(found[:, 2:3], (80, RAD)),
    ]
    shifted = [table] + [pltpu.roll(table, RAD - 8 * n, 1) for n in range(1, 4)]
    near = advance(shifted[0:2], 1, shifted[2], shifted[3], ghost, False)[0]
    lane1 = lax.broadcasted_iota(jnp.int32, (1, RAD), 1)
    for b in range(9):
        row = jnp.where(
            lane1 < SUBSTEPS, near[8 * b + 3 : 8 * b + 4], table[8 * b + 7 : 8 * b + 8]
        )
        there = jnp.broadcast_to(table[8 * b : 8 * b + 1, 32:33], (1, RAD)) > 0.0
        place = slice((b % 3) * RAD, (b % 3 + 1) * RAD)
        old = strength_ref[b // 3 : b // 3 + 1, place]
        new_ref[b // 3 : b // 3 + 1, place] = jnp.where(there, row, old)

    for copy in gather + halo + across + spread + rows:
        copy.wait_send()
    for g in range(PAIRS - 1):
        for n in range(2):
            to_z(g, n, partner).wait_send()
    to_z(PAIRS - 1, 0, partner).wait_send()


def hand_over(wall_ref, field_ref, new_ref, wall_out, field_out, new_out):
    wall_out[:, 0] = wall_ref[...]
    field_out[0] = field_ref[...]
    new_out[...] = new_ref[...]


def on_device(
    particle_position,
    particle_strength,
    core_radius,
    boundary_points,
    vorticity,
    swirl,
    diffusivity,
    intersection_source,
    intersection_target,
):
    prefactor = 1.6 / (4.0 * math.pi * math.sqrt(PART * NT * NY * NZ))
    vmem = pl.BlockSpec(memory_space=pltpu.VMEM)
    smem = pl.BlockSpec(memory_space=pltpu.SMEM)
    hbm = pl.BlockSpec(memory_space=pltpu.HBM)
    dma = pltpu.SemaphoreType.DMA
    wall, field, new = pl.pallas_call(
        lambda *refs: kernel(prefactor, *refs),
        out_shape=(
            jax.ShapeDtypeStruct((3, ANG), F32),
            jax.ShapeDtypeStruct((3, ANG, RAD), F32),
            jax.ShapeDtypeStruct((3, PART), F32),
        ),
        in_specs=[smem] * 2 + [hbm] * 7,
        out_specs=(vmem, vmem, vmem),
        scratch_shapes=[
            pltpu.VMEM((3, PART), F32),
            pltpu.VMEM((3, PART), F32),
            pltpu.VMEM((1, PART), F32),
            pltpu.VMEM((3, NY * NZ, ANG), F32),
            pltpu.VMEM((8, COLS), F32),
            pltpu.SMEM((4 * NT,), jnp.int32),
            pltpu.VMEM((NT, 8, PART), F32),
            pltpu.VMEM((64, COLS), BF16),
            pltpu.VMEM((NT * PART, 64), BF16),
            pltpu.VMEM((16, NT * PART), BF16),
            pltpu.VMEM((16, COLS), F32),
            pltpu.VMEM((5, 80, RAD), F32),
            pltpu.VMEM((PAIRS, NY, 4, 128), F32),
            pltpu.VMEM((NZ, NY, 4, 128), F32),
            pltpu.VMEM((NY, 4, 128), F32),
            pltpu.VMEM((NY, 4, 128), F32),
            pltpu.VMEM((4, 128), F32),
            pltpu.VMEM((NT, 4, 128), F32),
            pltpu.VMEM((80, RAD), F32),
            pltpu.VMEM((80, NT * ANG), BF16),
            pltpu.VMEM((3 * ANG, RAD), F32),
            pltpu.VMEM((2 * NT, 8, RAD), F32),
            pltpu.VMEM((2 * NT, 8, RAD), F32),
            dma((NT,)),
            dma((NT,)),
            dma((7,)),
            dma((6,)),
            dma((6,)),
            dma((NY,)),
            dma((NY,)),
            dma((NZ,)),
            dma((NZ,)),
            dma((NT,)),
            dma((NT,)),
            dma((NT,)),
            dma((NT,)),
        ],
        compiler_params=pltpu.CompilerParams(
            collective_id=0, has_side_effects=True, vmem_limit_bytes=67_000_000
        ),
        name="wake",
    )(
        intersection_target.reshape(-1),
        intersection_source.reshape(-1),
        particle_position,
        particle_strength,
        core_radius,
        boundary_points,
        vorticity.reshape(3, ANG, RAD),
        swirl.reshape(ANG, RAD),
        diffusivity.reshape(ANG, RAD),
    )
    return pl.pallas_call(
        hand_over,
        out_shape=(
            jax.ShapeDtypeStruct((3, 1, ANG), F32),
            jax.ShapeDtypeStruct((1, 3, ANG, RAD), F32),
            jax.ShapeDtypeStruct((3, PART), F32),
        ),
        in_specs=[vmem] * 3,
        out_specs=(vmem,) * 3,
        name="hand_over",
        compiler_params=pltpu.CompilerParams(vmem_limit_bytes=67_000_000),
    )(wall, field, new)


def solution(mesh):
    in_specs = (
        P(None, ("src", "tgt")),
        P(None, ("src", "tgt")),
        P(None, ("src", "tgt")),
        P(None, None, "tgt"),
        P("src", None, "tgt", None),
        P("src", "tgt", None),
        P("src", "tgt", None),
        P("src", "tgt", None),
        P("src", "tgt", None),
    )
    out_specs = (P(None, "src", "tgt"), P("src", None, "tgt", None), P(None, ("src", "tgt")))
    return jax.shard_map(
        on_device, mesh=mesh, in_specs=in_specs, out_specs=out_specs, check_vma=False
    )
```
